256 devices in a mesh: grp: 8 (over y, x_hi), row: 32 (over z, x_lo, core).
Axes of the slice: x: 4 (x_hi: 2, x_lo: 2; x = x_hi * 2 + x_lo), y: 4, z: 8, core: 2. Of those that a mesh axis runs over, the one named last changes fastest.
Arguments:
- features: float32 [32768, 256], P(('grp', 'row')), may hold values from -6 to 6
- adjacency_tiles: float32 [128, 8, 6, 256, 256], P('row', 'grp'), may hold values from -0.078125 to 0.078125
- tile_cols: int32 [128, 8, 6], P('row', 'grp'), may hold values from 0 to 15, as said below
- tile_count: int32 [128, 8], P('row', 'grp'), may hold values from 1 to 6, as said below
- weight: float32 [256, 256], replicated, may hold values from -0.375 to 0.375
- layer_bias: float32 [256], replicated, may hold values from -3 to 3
- cotangent: float32 [32768, 256], P('row'), may hold values from -6 to 6
Outputs:
- hidden_out: float32 [32768, 256], P('row')
- grad_features: float32 [32768, 256], P(('grp', 'row'))
- grad_weight: float32 [256, 256], replicated
- grad_bias: float32 [256], replicated
The draws below stay inside these ranges and needn't reach their ends.
Inputs may be any that keep to these rules, and one draw needn't show every extreme that they name: `tile_cols`: for each block row and column range the 6 slots name distinct column blocks. `tile_count`: in every column range some block row has all 6 slots live.
All inputs are finite; a program needn't handle non-finite values.
Results may differ from the reference program's by a relative error of at most 0.0003.
Values sent between devices are 32-bit elements; how exact they have to be, the bound alone decides.
A program may use at most 128 MiB of HBM per device.

```python
import jax
import jax.numpy as jnp
from jax import lax

F = 256
TILE = 256
TMAX = 6
NB = 128
CB = 16
NODES = 32768
N_GRP = 8


def draw_tile_cols(key, part):
    scores = jax.random.randint(key, (NB, N_GRP, CB), 0, 2 ** 20)
    keyed = scores * CB + lax.broadcasted_iota(jnp.int32, (NB, N_GRP, CB), 2)
    order = jnp.argsort(keyed, axis=-1, stable=True)
    return order[:, :, :TMAX].astype(jnp.int32)


def draw_tile_count(key, part):
    first = jax.random.fold_in(key, 11)
    second = jax.random.fold_in(key, 12)
    third = jax.random.fold_in(key, 13)
    base = jax.random.randint(first, (NB, N_GRP), 1, TMAX + 1)
    heavy = jax.random.randint(second, (NB, N_GRP), 0, 8) == 0
    counts = jnp.where(heavy, TMAX, base)
    chosen = jax.random.randint(third, (1, N_GRP), 0, NB)
    spots = lax.broadcasted_iota(jnp.int32, (NB, N_GRP), 0)
    counts = jnp.where(spots == chosen, TMAX, counts)
    return counts.astype(jnp.int32)


def shard_levels(own_key, extent, pieces, least, high):
    loudness, own = 1.0, jax.random.fold_in(own_key, 6)
    for axis_at, parts in pieces:
        steps = jnp.exp(jax.random.uniform(jax.random.fold_in(own, axis_at), (parts,), jnp.float32, least / len(pieces), high / len(pieces)))
        loudness = loudness * jnp.repeat(steps, extent[axis_at] // parts).reshape([-1 if axis == axis_at else 1 for axis in range(len(extent))])
    return loudness


def noise(key, dims, scale, reach, shards=(), held_as=jnp.bfloat16):
    entries = jax.random.normal(key, dims, jnp.float32) * scale
    if len(shards) > 0:
        entries = shard_levels(key, dims, shards, -0.22, 0.18) * entries
    return jnp.clip(entries, min=-reach, max=reach).astype(held_as)


def setup_inputs(seed: int = 0) -> dict:
    splits = jax.random.split(jax.random.key(seed), 8)
    features = noise(splits[0], (NODES, F), 1.0, 6.0, ((0, 256),), jnp.float32)
    adjacency_tiles = noise(splits[1], (NB, N_GRP, TMAX, TILE, TILE), (N_GRP * TMAX * TILE // 2) ** -0.5, 0.078125, ((0, 32), (1, 8)), jnp.float32)
    tile_cols = draw_tile_cols(jax.random.fold_in(splits[7], 71), 0)
    tile_count = draw_tile_count(jax.random.fold_in(splits[7], 71), 0)
    weight = noise(splits[4], (F, F), F ** -0.5, 0.375, (), jnp.float32)
    layer_bias = noise(splits[5], (F,), 0.5, 3.0, (), jnp.float32)
    cotangent = noise(splits[6], (NODES, F), 1.0, 6.0, ((0, 32),), jnp.float32)
    return dict(features=features, adjacency_tiles=adjacency_tiles, tile_cols=tile_cols, tile_count=tile_count, weight=weight, layer_bias=layer_bias, cotangent=cotangent)


def reference(features, adjacency_tiles, tile_cols, tile_count, weight, layer_bias, cotangent):
    highest = lax.Precision.HIGHEST
    block_total, groups, slot_count, tile_size, _ = adjacency_tiles.shape
    width = features.shape[1]
    range_blocks = features.shape[0] // (groups * tile_size)
    columns = features.reshape(groups, range_blocks, tile_size, width)
    group_ids = jnp.arange(groups, dtype=jnp.int32)[:, None]
    slot_ids = jnp.arange(slot_count, dtype=jnp.int32)[None, :]
    block_ids = jnp.arange(range_blocks, dtype=jnp.int32)

    def live_mask(index):
        return (slot_ids < tile_count[index][:, None]).astype(jnp.float32)

    def forward_row(index):
        chosen = columns[group_ids, tile_cols[index]] * live_mask(index)[:, :, None, None]
        return jnp.einsum('gsij,gsjf->if', adjacency_tiles[index], chosen, precision=highest)
    summed = lax.map(forward_row, jnp.arange(block_total, dtype=jnp.int32)).reshape(block_total * tile_size, width)
    preact = jnp.dot(summed, weight, precision=highest) + layer_bias
    sigma = jax.nn.sigmoid(preact)
    hidden_out = preact * sigma
    grad_pre = cotangent * sigma * (1.0 + preact * (1.0 - sigma))
    scaling = 1.0 / jnp.sqrt(jnp.float32(block_total * tile_size))
    grad_weight = jnp.dot(summed.T, grad_pre, precision=highest) * scaling
    grad_bias = lax.optimization_barrier(jnp.sum(grad_pre, axis=0)) * scaling
    backward = jnp.dot(grad_pre, weight.T, precision=highest).reshape(block_total, tile_size, width)

    def accumulate(total, index):
        spread = jnp.einsum('gsij,if->gsjf', adjacency_tiles[index], backward[index], precision=highest)
        picks = (tile_cols[index][:, :, None] == block_ids[None, None, :]).astype(jnp.float32) * live_mask(index)[:, :, None]
        return (total + jnp.einsum('gsc,gsjf->gcjf', picks, spread, precision=highest), None)
    start = jnp.zeros((groups, range_blocks, tile_size, width), jnp.float32)
    grad_cols, _ = lax.scan(accumulate, start, jnp.arange(block_total, dtype=jnp.int32))
    grad_features = grad_cols.reshape(groups * range_blocks * tile_size, width)
    return (hidden_out, grad_features, grad_weight, grad_bias)
```

```python
import functools

import jax
import jax.numpy as jnp
from jax import lax
from jax.experimental import pallas as pl
from jax.experimental.pallas import tpu as pltpu
from jax.sharding import PartitionSpec as P

MESH = pl.DeviceIdType.MESH
F32, BF16 = jnp.float32, jnp.bfloat16
NZ, NY = 8, 4
T = 256
AG_Q = 56
RS_Q = 112
N_MSG = 160


def split(x):
    hi = x.astype(BF16)
    return hi, (x - hi.astype(F32)).astype(BF16)


def dot(a, b, ca=1, cb=0):
    return lax.dot_general(a, b, (((ca,), (cb,)), ((), ())), preferred_element_type=F32)


def dot3(a, b, ca=1, cb=0):
    (ah, al), (bh, bl) = a, b
    return dot(ah, bh, ca, cb) + dot(ah, bl, ca, cb) + dot(al, bh, ca, cb)


def kernel(
    scaling,
    feat, tiles, cols, counts, weight, bias, cot,
    hid_out, gf_out, gw_out, gb_out,
    panel, stage, a_hi, a_lo, x_hi, x_lo, w_hi, w_lo, cot_v,
    part, y1, y2, ysum, arx, agg, hid, gw_acc, gb_acc,
    spread, g_send, g_own, g_recv, rx, le, lq, xq,
    gwp, g1, g2, r3, gwo, inv, msk,
    send_sem, recv_sem, load_sem,
):
    row, grp = lax.axis_index("row"), lax.axis_index("grp")
    z, xl, c = lax.div(row, 4), lax.rem(lax.div(row, 2), 2), lax.rem(row, 2)
    y, xh = lax.div(grp, 2), lax.rem(grp, 2)

    def zz(k):
        return lax.rem(z + (k + NZ), NZ)

    def yy(k):
        return lax.rem(y + (k + NY), NY)

    def dev(z_=None, xl_=None, c_=None, y_=None, xh_=None):
        z_, xl_, c_ = z if z_ is None else z_, xl if xl_ is None else xl_, c if c_ is None else c_
        y_, xh_ = y if y_ is None else y_, xh if xh_ is None else xh_
        return {"grp": y_ * 2 + xh_, "row": z_ * 4 + xl_ * 2 + c_}

    def blk(z_, xl_, c_):
        return z_ * 4 + xl_ * 2 + c_

    def m8(v):
        return pl.multiple_of(v, 8)

    msgs = {}

    def push(key, src, dst, device):
        at = len(msgs)
        copy = pltpu.make_async_remote_copy(
            src_ref=src, dst_ref=dst, send_sem=send_sem.at[at], recv_sem=recv_sem.at[at],
            device_id=device, device_id_type=MESH,
        )
        copy.start()
        msgs[key] = copy

    def take(key):
        msgs[key].wait_recv()

    loads = [pltpu.make_async_copy(tiles.at[b, 0], stage.at[b], load_sem.at[b]) for b in range(4)]
    for load in loads:
        load.start()
    cot_load = pltpu.make_async_copy(cot, cot_v, load_sem.at[4])
    cot_load.start()

    barrier = pltpu.get_barrier_semaphore()
    peers = [dev(z_=zz(k)) for k in range(1, NZ)] + [dev(y_=yy(k)) for k in range(1, NY)]
    peers += [dev(xl_=1 - xl), dev(xh_=1 - xh), dev(xl_=1 - xl, xh_=1 - xh), dev(c_=1 - c)]
    for peer in peers:
        pl.semaphore_signal(barrier, inc=1, device_id=peer, device_id_type=MESH)

    own = blk(z, xl, c)
    panel[own] = feat[...]
    wh, wl = split(weight[...])
    w_hi[...] = wh
    w_lo[...] = wl
    pl.semaphore_wait(barrier, len(peers))

    up, down, across, twin = dev(z_=zz(1)), dev(z_=zz(-1)), dev(xl_=1 - xl), dev(c_=1 - c)
    along = {1: up, -1: down}
    for d in (1, -1):
        push(("E", d, 1), feat, panel.at[own], along[d])
    push(("Q", 0), feat.at[pl.ds(0, AG_Q)], panel.at[own, pl.ds(0, AG_Q)], across)
    push(("P", 0), feat.at[pl.ds(AG_Q, 128 - AG_Q)], panel.at[own, pl.ds(AG_Q, 128 - AG_Q)], across)
    push(("SE", 0), feat, panel.at[own], twin)

    def same(key, at, first, count, device):
        ref = panel.at[at, pl.ds(first, count)]
        push(key, ref, ref, device)

    def prepare_tables():
        @pl.loop(0, 64)
        def _(i):
            b, col = lax.div(i, 16), lax.rem(i, 16)
            slot, live = jnp.int32(0), jnp.float32(0)
            for t in range(6):
                hit = jnp.logical_and(cols[b, 0, t] == col, counts[b, 0] > t)
                slot = jnp.where(hit, b * 6 + t, slot)
                live = jnp.where(hit, jnp.float32(1), live)
            inv[i] = slot
            msk[i] = live

    def prepare(b):
        loads[b].wait()
        for t in range(6):
            hi, lo = split(stage[b, t])
            a_hi[b, :, pl.ds(t * T, T)] = hi
            a_lo[b, :, pl.ds(t * T, T)] = lo

    prepare_tables()
    take(("Q", 0))
    for d in (1, -1):
        same(("Q", d, 1), blk(z, 1 - xl, c), 0, AG_Q, along[d])

    q_half = {1: (0, 32), -1: (32, AG_Q - 32)}
    for k in (1, 2, 3):
        for d in (1, -1):
            at = blk(zz(-d * k), xl, c)
            take(("E", d, k))
            if k < 3:
                same(("E", d, k + 1), at, 0, 128, along[d])
            else:
                same(("E", d, 4), at, 0 if d == 1 else 64, 64, along[d])
            same(("P", d * k), at, AG_Q, 128 - AG_Q, across)
            same(("SE", d * k), at, 0, 128, twin)
        for d in (1, -1):
            at = blk(zz(-d * k), 1 - xl, c)
            take(("Q", d, k))
            if k < 3:
                same(("Q", d, k + 1), at, 0, AG_Q, along[d])
            else:
                same(("Q", d, 4), at, *q_half[d], along[d])
        for o in ((0,) if k == 1 else (k - 1, 1 - k)):
            take(("P", o))
            same(("SQ", o), blk(zz(-o), 1 - xl, c), 0, 128, twin)
        prepare(k - 1)
    at = blk(zz(4), xl, c)
    take(("E", 1, 4))
    take(("E", -1, 4))
    same(("P", 4), at, AG_Q, 128 - AG_Q, across)
    same(("SE", 4), at, 0, 128, twin)
    for o in (3, -3):
        take(("P", o))
        same(("SQ", o), blk(zz(-o), 1 - xl, c), 0, 128, twin)
    take(("Q", 1, 4))
    take(("Q", -1, 4))
    prepare(3)
    take(("P", 4))
    same(("SQ", 4), blk(zz(4), 1 - xl, c), 0, 128, twin)
    for o in (0, 1, -1, 2, -2, 3, -3, 4):
        take(("SE", o))
        take(("SQ", o))

    def forward(b):
        for t in range(6):
            at = cols[b, 0, t]
            live = jnp.where(counts[b, 0] > t, jnp.float32(1), jnp.float32(0))
            hi, lo = split(panel[pl.ds(2 * at, 2)].reshape(T, T) * live)
            x_hi[pl.ds(t * T, T), :] = hi
            x_lo[pl.ds(t * T, T), :] = lo
        part[pl.ds(b * T, T), :] = dot3((a_hi[b], a_lo[b]), (x_hi[...], x_lo[...]))

    ahead, behind, opposite = dev(y_=yy(1)), dev(y_=yy(-1)), dev(xh_=1 - xh)

    def rows(b, k, first, count):
        return pl.ds(m8(b * T + yy(k) * 64 + first), count)

    for b in range(4):
        forward(b)
        push(("Y1", 1, b), part.at[rows(b, 2, 0, 32)], y1.at[b, 0], ahead)
        push(("Y1", -1, b), part.at[rows(b, 2, 32, 32)], y1.at[b, 1], behind)
    for b in range(4):
        take(("Y1", 1, b))
        part[rows(b, 1, 0, 32)] += y1[b, 0]
        push(("Y2", 1, b), part.at[rows(b, 1, 0, 64)], y2.at[b, 0], ahead)
        take(("Y1", -1, b))
        part[rows(b, -1, 32, 32)] += y1[b, 1]
        push(("Y2", -1, b), part.at[rows(b, -1, 0, 64)], y2.at[b, 1], behind)
    for b in range(4):
        take(("Y2", 1, b))
        take(("Y2", -1, b))
        ysum[b] = part[rows(b, 0, 0, 64)] + y2[b, 0] + y2[b, 1]
        push(("X", b), ysum.at[b], arx.at[b], opposite)
    for b in range(4):
        take(("X", b))
        agg[rows(b, 0, 0, 64)] = ysum[b] + arx[b]
        mine = agg.at[rows(b, 0, 0, 64)]
        push(("Y3", 1, b), mine, mine, ahead)
        push(("Y3", -1, b), mine, mine, behind)
    for b in range(4):
        take(("Y3", 1, b))
        ref = agg.at[rows(b, -1, 0, 32)]
        push(("Y4", 1, b), ref, ref, ahead)
        take(("Y3", -1, b))
        ref = agg.at[rows(b, 1, 32, 32)]
        push(("Y4", -1, b), ref, ref, behind)

    cot_load.wait()
    stores = []
    for b in range(4):
        take(("Y4", 1, b))
        take(("Y4", -1, b))
        span = pl.ds(b * T, T)
        summed = agg[span, :]
        w = (w_hi[...], w_lo[...])
        pre = dot3(split(summed), w) + bias[...]
        sigma = jax.nn.sigmoid(pre)
        hid[span, :] = pre * sigma
        store = pltpu.make_async_copy(hid.at[span], hid_out.at[span], load_sem.at[5 + b])
        store.start()
        stores.append(store)
        grad = cot_v[span, :] * sigma * (1.0 + pre * (1.0 - sigma))
        gs = split(grad)
        gw = dot3(split(summed.T), gs)
        gb = jnp.sum(grad, axis=0, keepdims=True)
        gw_acc[...] = gw if b == 0 else gw_acc[...] + gw
        gb_acc[...] = gb if b == 0 else gb_acc[...] + gb
        bh, bl = split(dot3(w, gs, 1, 1))
        for t in range(6):
            tile = pl.ds(t * T, T)
            sp = dot3((bh, bl), (a_hi[b, :, tile], a_lo[b, :, tile]))
            spread[b * 6 + t, 0] = sp[:, :128]
            spread[b * 6 + t, 1] = sp[:, 128:]

    gwp[...] = jnp.zeros_like(gwp)
    for c_ in range(2):
        for xl_ in range(2):
            piece = gw_acc[pl.ds(m8(grp * 32 + (xl_ * 2 + c_) * 8), 8), :]
            gwp[c_, xl_, :, pl.ds(0, 256)] = piece * scaling
            gwp[c_, xl_, pl.ds(0, 1), pl.ds(256, 128)] = gb_acc[:, pl.ds(0, 128)] * scaling
            gwp[c_, xl_, pl.ds(1, 1), pl.ds(256, 128)] = gb_acc[:, pl.ds(128, 128)] * scaling
    push(("G1",), gwp.at[1 - c], g1, twin)

    def gather(col, half):
        total = None
        for b in range(4):
            at = b * 16 + col
            term = spread[inv[at], half] * msk[at]
            total = term if total is None else total + term
        return total

    order = (4, 3, -3, 2, -2, 1, -1, 0)
    slot_of = {o: i for i, o in enumerate(order)}

    def col_of(o, other):
        return zz(o) * 2 + ((1 - xl) if other else xl)

    for o in order:
        for other in (True, False):
            col = col_of(o, other)
            g_send[col] = gather(col, 1 - c)
            push(("S", o, other), g_send.at[col], g_recv.at[col], twin)

    p_rows = pl.ds(RS_Q, T - RS_Q)

    def chip_sum(o):
        for other in (True, False):
            col = col_of(o, other)
            mine = gather(col, c)
            take(("S", o, other))
            g_own[col] = mine + g_recv[col]
            if other:
                push(("RX", o), g_own.at[col, p_rows], rx.at[slot_of[o]], across)

    e_half = {1: pl.ds(0, 128), -1: pl.ds(128, 128)}
    r_half = {1: pl.ds(0, 56), -1: pl.ds(56, 56)}

    def ring(k):
        for d in (1, -1):
            col = col_of(d * k, True)
            span = r_half[d] if k == 4 else pl.ds(0, RS_Q)
            if k < 4:
                take(("RQ", d, k + 1))
                got = r_half[d] if k == 3 else span
                g_own[col, got] += lq[0 if d == 1 else 1, k, got]
            push(("RQ", d, k), g_own.at[col, span], lq.at[0 if d == 1 else 1, k - 1, span], along[d])
        for d in (1, -1):
            col = col_of(d * k, False)
            if k < 4 or d == 1:
                take(("RX", d * k))
                g_own[col, p_rows] += rx[slot_of[d * k]]
            span = e_half[d] if k == 4 else pl.ds(0, T)
            if k < 4:
                take(("RE", d, k + 1))
                got = e_half[d] if k == 3 else span
                g_own[col, got] += le[0 if d == 1 else 1, k, got]
            push(("RE", d, k), g_own.at[col, span], le.at[0 if d == 1 else 1, k - 1, span], along[d])

    chip_sum(4)
    chip_sum(3)
    chip_sum(-3)
    ring(4)
    take(("G1",))
    gwp[c] += g1[...]
    push(("G2",), gwp.at[c, 1 - xl], g2, across)
    chip_sum(2)
    chip_sum(-2)
    ring(3)
    take(("G2",))
    r3[z] = gwp[c, xl] + g2[...]
    for k in range(1, NZ):
        push(("G3", k), r3.at[z], r3.at[z], dev(z_=zz(k)))
    chip_sum(1)
    chip_sum(-1)
    chip_sum(0)
    ring(2)
    for k in range(1, NZ):
        take(("G3", k))
    fin = r3[0]
    for k in range(1, NZ):
        fin = fin + r3[k]
    gb_out[:, pl.ds(0, 128)] = fin[0:1, 256:]
    gb_out[:, pl.ds(128, 128)] = fin[1:2, 256:]
    gwo[y, xh, xl, c] = fin[:, :256]
    for k in range(1, NY):
        ref = gwo.at[y, xh, xl, c]
        push(("G4", k), ref, ref, dev(y_=yy(k)))
    ring(1)
    for k in range(1, NY):
        take(("G4", k))
    for i, (a, b) in enumerate(((0, 1), (1, 0), (1, 1))):
        ref = gwo.at[:, xh, xl, c]
        push(("G5", i), ref, ref, dev(xh_=(1 - xh) if a else xh, xl_=(1 - xl) if b else xl))

    col = col_of(0, True)
    q_rows = pl.ds(0, RS_Q)
    for d in (1, -1):
        take(("RQ", d, 1))
        g_own[col, q_rows] += lq[0 if d == 1 else 1, 0, q_rows]
    push(("XF",), g_own.at[col, q_rows], xq, across)
    for i in range(3):
        take(("G5", i))
    ref = gwo.at[:, :, :, c]
    push(("G6",), ref, ref, twin)
    col = col_of(0, False)
    take(("RX", 0))
    g_own[col, p_rows] += rx[slot_of[0]]
    for d in (1, -1):
        take(("RE", d, 1))
    total = g_own[col] + le[0, 0] + le[1, 0]
    g_own[col] = total
    take(("XF",))
    g_own[col, q_rows] += xq[...]
    gf_out[...] = g_own[col].T
    take(("G6",))
    gw_out[...] = gwo[...].reshape(256, 256)

    for store in stores:
        store.wait()
    for copy in msgs.values():
        copy.wait_send()


def on_device(features, tiles, cols, counts, weight, bias, cot):
    n_rows = cot.shape[0]
    scaling = 1.0 / float(n_rows * 32) ** 0.5
    vmem = pl.BlockSpec(memory_space=pltpu.VMEM)
    smem = pl.BlockSpec(memory_space=pltpu.SMEM)
    hbm = pl.BlockSpec(memory_space=pl.ANY)
    shape = jax.ShapeDtypeStruct
    V = pltpu.VMEM
    scratch = [
        V((32, 128, T), F32),
        V((4, 6, T, T), F32),
        V((4, T, 6 * T), BF16), V((4, T, 6 * T), BF16),
        V((6 * T, T), BF16), V((6 * T, T), BF16),
        V((T, T), BF16), V((T, T), BF16),
        V((1024, T), F32),
        V((1024, T), F32),
        V((4, 2, 32, T), F32), V((4, 2, 64, T), F32),
        V((4, 64, T), F32), V((4, 64, T), F32),
        V((1024, T), F32), V((1024, T), F32),
        V((T, T), F32), V((1, T), F32),
        V((24, 2, T, 128), F32),
        V((16, T, 128), F32), V((16, T, 128), F32), V((16, T, 128), F32),
        V((8, T - RS_Q, 128), F32),
        V((2, 4, T, 128), F32), V((2, 4, RS_Q, 128), F32),
        V((RS_Q, 128), F32),
        V((2, 2, 8, 384), F32), V((2, 8, 384), F32), V((8, 384), F32),
        V((8, 8, 384), F32),
        V((4, 2, 2, 2, 8, T), F32),
        pltpu.SMEM((64,), jnp.int32), pltpu.SMEM((64,), F32),
        pltpu.SemaphoreType.DMA((N_MSG,)), pltpu.SemaphoreType.DMA((N_MSG,)),
        pltpu.SemaphoreType.DMA((16,)),
    ]
    hid, gf, gw, gb = pl.pallas_call(
        functools.partial(kernel, scaling),
        out_shape=(
            shape((1024, T), F32), shape((128, T), F32), shape((T, T), F32), shape((1, T), F32),
        ),
        in_specs=[vmem, hbm, smem, smem, vmem, vmem, hbm],
        out_specs=(hbm, vmem, vmem, vmem),
        scratch_shapes=scratch,
        compiler_params=pltpu.CompilerParams(
            collective_id=0, has_side_effects=True, vmem_limit_bytes=60 << 20,
        ),
        name="graph_layer",
    )(features, tiles, cols, counts, weight, bias.reshape(1, T), cot)
    return hid, gf, gw, gb.reshape(T)


def solution(mesh):
    return jax.shard_map(
        on_device,
        mesh=mesh,
        in_specs=(
            P(("grp", "row"), None),
            P("row", "grp", None, None, None),
            P("row", "grp", None),
            P("row", "grp"),
            P(),
            P(),
            P("row", None),
        ),
        out_specs=(P("row", None), P(("grp", "row"), None), P(), P()),
        check_vma=False,
    )
```

```python
import functools

import jax
import jax.numpy as jnp
from jax import lax
from jax.experimental import pallas as pl
from jax.experimental.pallas import tpu as pltpu
from jax.sharding import PartitionSpec as P

MESH = pl.DeviceIdType.MESH
F32, BF16 = jnp.float32, jnp.bfloat16
NZ, NY = 8, 4
T = 256
AG_Q = 56
RS_Q = 112
N_MSG = 240


def split(x):
    hi = x.astype(BF16)
    return hi, (x - hi.astype(F32)).astype(BF16)


def dot(a, b, ca=1, cb=0):
    return lax.dot_general(a, b, (((ca,), (cb,)), ((), ())), preferred_element_type=F32)


def dot3(a, b, ca=1, cb=0):
    (ah, al), (bh, bl) = a, b
    return dot(ah, bh, ca, cb) + dot(ah, bl, ca, cb) + dot(al, bh, ca, cb)


def kernel(
    scaling,
    feat, tiles, cols_in, counts_in, weight, bias_in, cot,
    hid_out, gf_out, gw_out, gb_out,
    panel_a, panel_b, stage, a_hi, a_lo, x_hi, x_lo, w_v, w_hi, w_lo, bias, cot_v,
    part, y1, y2, ysum, arx, agg, hid, gw_acc, gb_acc,
    spread, g_send, g_own, g_recv, rx, le, lq, xq,
    gwp, g1, g2, r3, gwo, cols, counts, inv, msk,
    send_sem, recv_sem, load_sem,
):
    row, grp = lax.axis_index("row"), lax.axis_index("grp")
    z, xl, c = lax.div(row, 4), lax.rem(lax.div(row, 2), 2), lax.rem(row, 2)
    y, xh = lax.div(grp, 2), lax.rem(grp, 2)

    def zz(k):
        return lax.rem(z + (k + NZ), NZ)

    def yy(k):
        return lax.rem(y + (k + NY), NY)

    def dev(z_=None, xl_=None, c_=None, y_=None, xh_=None):
        z_, xl_, c_ = z if z_ is None else z_, xl if xl_ is None else xl_, c if c_ is None else c_
        y_, xh_ = y if y_ is None else y_, xh if xh_ is None else xh_
        return {"grp": y_ * 2 + xh_, "row": z_ * 4 + xl_ * 2 + c_}

    def blk(z_, xl_, c_):
        return z_ * 4 + xl_ * 2 + c_

    def m8(v):
        return pl.multiple_of(v, 8)

    panels = (panel_a, panel_b)
    msgs = {}

    def push(key, src, dst, device):
        at = len(msgs)
        copy = pltpu.make_async_remote_copy(
            src_ref=src, dst_ref=dst, send_sem=send_sem.at[at], recv_sem=recv_sem.at[at],
            device_id=device, device_id_type=MESH,
        )
        copy.start()
        msgs[key] = copy

    def take(key):
        msgs[key].wait_recv()

    own = blk(z, xl, c)
    n_loads = [0]

    def load(src, dst):
        copy = pltpu.make_async_copy(src, dst, load_sem.at[n_loads[0]])
        copy.start()
        n_loads[0] += 1
        return copy

    barrier = pltpu.get_barrier_semaphore()
    peers = [dev(z_=zz(k)) for k in range(1, NZ)] + [dev(y_=yy(k)) for k in range(1, NY)]
    peers += [dev(xl_=1 - xl), dev(xh_=1 - xh), dev(xl_=1 - xl, xh_=1 - xh), dev(c_=1 - c)]
    for peer in peers:
        pl.semaphore_signal(barrier, inc=1, device_id=peer, device_id_type=MESH)

    feat_loads = [load(feat.at[:, pl.ds(h * 128, 128)], panels[h].at[own]) for h in range(2)]
    small_loads = [load(cols_in, cols), load(counts_in, counts), load(weight, w_v), load(bias_in, bias)]
    tile_loads = [load(tiles.at[b, 0], stage.at[b]) for b in range(4)]
    cot_load = load(cot, cot_v)
    for copy in feat_loads:
        copy.wait()
    pl.semaphore_wait(barrier, len(peers))

    up, down, across, twin = dev(z_=zz(1)), dev(z_=zz(-1)), dev(xl_=1 - xl), dev(c_=1 - c)
    along = {1: up, -1: down}
    both = (1, -1)
    AG_P = 128 - AG_Q
    ep_half = {1: (AG_Q, 40), -1: (AG_Q + 40, AG_P - 40)}
    eq_half = {1: (0, 32), -1: (32, AG_Q - 32)}

    def same(h, key, at, span, device):
        ref = panels[h].at[at, pl.ds(*span)]
        push((h, *key), ref, ref, device)

    def ag_init(h):
        for d in both:
            same(h, ("EP", d, 1), own, (AG_Q, AG_P), along[d])
        same(h, ("Q", 0), own, (0, AG_Q), across)
        for d in both:
            same(h, ("EQ", d, 1), own, (0, AG_Q), along[d])
        same(h, ("P", 0), own, (AG_Q, AG_P), across)
        same(h, ("SE", 0), own, (0, 128), twin)

    def ag_q0(h):
        take((h, "Q", 0))
        for d in both:
            same(h, ("Q", d, 1), blk(z, 1 - xl, c), (0, AG_Q), along[d])

    def ag_crossed(h, o):
        take((h, "P", o))
        same(h, ("SQ", o), blk(zz(-o), 1 - xl, c), (0, 128), twin)

    def ag_hop(h, k):
        for d in both:
            at = blk(zz(-d * k), xl, c)
            take((h, "EP", d, k))
            same(h, ("EP", d, k + 1), at, (AG_Q, AG_P) if k < 3 else ep_half[d], along[d])
            same(h, ("P", d * k), at, (AG_Q, AG_P), across)
        for d in both:
            at = blk(zz(-d * k), xl, c)
            take((h, "EQ", d, k))
            same(h, ("EQ", d, k + 1), at, (0, AG_Q) if k < 3 else eq_half[d], along[d])
            same(h, ("SE", d * k), at, (0, 128), twin)
        for d in both:
            at = blk(zz(-d * k), 1 - xl, c)
            take((h, "Q", d, k))
            same(h, ("Q", d, k + 1), at, (0, AG_Q) if k < 3 else eq_half[d], along[d])
        for o in ((0,) if k == 1 else (k - 1, 1 - k)):
            ag_crossed(h, o)

    def ag_last(h):
        at = blk(zz(4), xl, c)
        for d in both:
            take((h, "EP", d, 4))
        same(h, ("P", 4), at, (AG_Q, AG_P), across)
        for d in both:
            take((h, "EQ", d, 4))
        same(h, ("SE", 4), at, (0, 128), twin)
        ag_crossed(h, 3)
        ag_crossed(h, -3)
        for d in both:
            take((h, "Q", d, 4))

    def ag_end(h):
        ag_crossed(h, 4)
        for o in (0, 1, -1, 2, -2, 3, -3, 4):
            take((h, "SE", o))
            take((h, "SQ", o))

    def prepare_tables():
        for copy in small_loads:
            copy.wait()
        wh, wl = split(w_v[...])
        w_hi[...] = wh
        w_lo[...] = wl

        @pl.loop(0, 64)
        def _(i):
            b, col = lax.div(i, 16), lax.rem(i, 16)
            slot, live = jnp.int32(0), jnp.float32(0)
            for t in range(6):
                hit = jnp.logical_and(cols[b, 0, t] == col, counts[0, b] > t)
                slot = jnp.where(hit, b * 6 + t, slot)
                live = jnp.where(hit, jnp.float32(1), live)
            inv[i] = slot
            msk[i] = live

    def prepare(b):
        tile_loads[b].wait()
        for t in range(6):
            hi, lo = split(stage[b, t])
            a_hi[b, :, pl.ds(t * T, T)] = hi
            a_lo[b, :, pl.ds(t * T, T)] = lo

    def forward(h, b):
        for t in range(6):
            at = cols[b, 0, t]
            live = jnp.where(counts[0, b] > t, jnp.float32(1), jnp.float32(0))
            hi, lo = split(panels[h][pl.ds(2 * at, 2)].reshape(T, 128) * live)
            x_hi[pl.ds(t * T, T), :] = hi
            x_lo[pl.ds(t * T, T), :] = lo
        part[h, pl.ds(b * T, T), :] = dot3((a_hi[b], a_lo[b]), (x_hi[...], x_lo[...]))

    ahead, behind, opposite = dev(y_=yy(1)), dev(y_=yy(-1)), dev(xh_=1 - xh)

    def rows(b, k, first, count):
        return pl.ds(m8(b * T + yy(k) * 64 + first), count)

    def s1(h, b):
        forward(h, b)
        push((h, "Y1", 1, b), part.at[h, rows(b, 2, 0, 32)], y1.at[h, b, 0], ahead)
        push((h, "Y1", -1, b), part.at[h, rows(b, 2, 32, 32)], y1.at[h, b, 1], behind)

    def s2(h, b):
        take((h, "Y1", 1, b))
        part[h, rows(b, 1, 0, 32)] += y1[h, b, 0]
        push((h, "Y2", 1, b), part.at[h, rows(b, 1, 0, 64)], y2.at[h, b, 0], ahead)
        take((h, "Y1", -1, b))
        part[h, rows(b, -1, 32, 32)] += y1[h, b, 1]
        push((h, "Y2", -1, b), part.at[h, rows(b, -1, 0, 64)], y2.at[h, b, 1], behind)

    def s3(h, b):
        take((h, "Y2", 1, b))
        take((h, "Y2", -1, b))
        ysum[h, b] = part[h, rows(b, 0, 0, 64)] + y2[h, b, 0] + y2[h, b, 1]
        push((h, "X", b), ysum.at[h, b], arx.at[h, b], opposite)

    def s4(h, b):
        take((h, "X", b))
        agg[h, rows(b, 0, 0, 64)] = ysum[h, b] + arx[h, b]
        mine = agg.at[h, rows(b, 0, 0, 64)]
        push((h, "Y3", 1, b), mine, mine, ahead)
        push((h, "Y3", -1, b), mine, mine, behind)

    def s5(h, b):
        take((h, "Y3", 1, b))
        ref = agg.at[h, rows(b, -1, 0, 32)]
        push((h, "Y4", 1, b), ref, ref, ahead)
        take((h, "Y3", -1, b))
        ref = agg.at[h, rows(b, 1, 32, 32)]
        push((h, "Y4", -1, b), ref, ref, behind)

    def s6(h, b):
        take((h, "Y4", 1, b))
        take((h, "Y4", -1, b))

    stores = []

    def dense(b):
        span = pl.ds(b * T, T)
        summed = jnp.concatenate([agg[0, span], agg[1, span]], axis=1)
        w = (w_hi[...], w_lo[...])
        pre = dot3(split(summed), w) + bias[...]
        sigma = jax.nn.sigmoid(pre)
        hid[span, :] = pre * sigma
        stores.append(load(hid.at[span], hid_out.at[span]))
        grad = cot_v[span, :] * sigma * (1.0 + pre * (1.0 - sigma))
        gs = split(grad)
        bh, bl = split(dot3(w, gs, 1, 1))
        for t in range(6):
            tile = pl.ds(t * T, T)
            sp = dot3((bh, bl), (a_hi[b, :, tile], a_lo[b, :, tile]))
            spread[b * 6 + t, 0] = sp[:, :128]
            spread[b * 6 + t, 1] = sp[:, 128:]
        gw = dot3(split(summed.T), gs)
        gb = jnp.sum(grad, axis=0, keepdims=True)
        gw_acc[...] = gw if b == 0 else gw_acc[...] + gw
        gb_acc[...] = gb if b == 0 else gb_acc[...] + gb

    ag_init(0)
    prepare_tables()
    ag_q0(0)
    ag_init(1)
    ag_hop(0, 1)
    prepare(0)
    ag_q0(1)
    ag_hop(0, 2)
    ag_hop(1, 1)
    prepare(1)
    ag_hop(0, 3)
    ag_hop(1, 2)
    prepare(2)
    ag_last(0)
    ag_hop(1, 3)
    prepare(3)
    ag_end(0)
    s1(0, 0)
    s1(0, 1)
    ag_last(1)
    s1(0, 2)
    s1(0, 3)
    s2(0, 0)
    s2(0, 1)
    ag_end(1)
    for b in range(4):
        s1(1, b)
        if b < 2:
            s2(0, b + 2)
        if b >= 2:
            s3(0, 2 * b - 4)
            s3(0, 2 * b - 3)
    for b in range(4):
        s4(0, b)
        s2(1, b)
    for b in range(4):
        s5(0, b)
        s3(1, b)
    for b in range(4):
        s4(1, b)
    for b in range(4):
        s6(0, b)
        s5(1, b)
    cot_load.wait()
    for b in range(4):
        s6(1, b)
        dense(b)

    gwp[...] = jnp.zeros_like(gwp)
    for c_ in range(2):
        for xl_ in range(2):
            piece = gw_acc[pl.ds(m8(grp * 32 + (xl_ * 2 + c_) * 8), 8), :]
            gwp[c_, xl_, :, pl.ds(0, 256)] = piece * scaling
            gwp[c_, xl_, pl.ds(0, 1), pl.ds(256, 128)] = gb_acc[:, pl.ds(0, 128)] * scaling
            gwp[c_, xl_, pl.ds(1, 1), pl.ds(256, 128)] = gb_acc[:, pl.ds(128, 128)] * scaling
    push(("G1",), gwp.at[1 - c], g1, twin)

    def gather(col, half):
        total = None
        for b in range(4):
            at = b * 16 + col
            term = spread[inv[at], half] * msk[at]
            total = term if total is None else total + term
        return total

    slot_of = {o: i for i, o in enumerate((4, 3, -3, 2, -2, 1, -1, 0))}
    lane_of = {1: 0, -1: 1}
    RS_P = T - RS_Q
    p_rows, q_rows = pl.ds(RS_Q, RS_P), pl.ds(0, RS_Q)

    def col_of(o, other):
        return zz(o) * 2 + ((1 - xl) if other else xl)

    def to_twin(o):
        for other in (True, False):
            col = col_of(o, other)
            g_send[col] = gather(col, 1 - c)
            push(("S", o, other), g_send.at[col], g_recv.at[col], twin)

    def chip_sum(o):
        for other in (True, False):
            col = col_of(o, other)
            mine = gather(col, c)
            take(("S", o, other))
            g_own[col] = mine + g_recv[col]
            if other:
                push(("RX", o), g_own.at[col, p_rows], rx.at[slot_of[o]], across)

    q_part = {1: pl.ds(0, 56), -1: pl.ds(56, 56)}
    p_part = {1: pl.ds(RS_Q, 72), -1: pl.ds(RS_Q + 72, 72)}

    def ring_q(k):
        for other, name, land in ((True, "RQ", lq), (False, "REQ", le)):
            for d in both:
                col = col_of(d * k, other)
                if k < 4:
                    take((name, d, k + 1))
                    got = q_part[d] if k == 3 else q_rows
                    g_own[col, got] += land[lane_of[d], k, got]
                span = q_part[d] if k == 4 else q_rows
                push((name, d, k), g_own.at[col, span], land.at[lane_of[d], k - 1, span], along[d])

    def ring_p(k):
        for d in both:
            col = col_of(d * k, False)
            if k < 4 or d == 1:
                take(("RX", d * k))
                g_own[col, p_rows] += rx[slot_of[d * k]]
            if k < 4:
                take(("REP", d, k + 1))
                got = p_part[d] if k == 3 else p_rows
                g_own[col, got] += le[lane_of[d], k, got]
            span = p_part[d] if k == 4 else p_rows
            push(("REP", d, k), g_own.at[col, span], le.at[lane_of[d], k - 1, span], along[d])

    to_twin(4)
    to_twin(3)
    to_twin(-3)
    chip_sum(4)
    ring_q(4)
    to_twin(2)
    to_twin(-2)
    chip_sum(3)
    chip_sum(-3)
    ring_p(4)
    to_twin(1)
    to_twin(-1)
    to_twin(0)
    take(("G1",))
    gwp[c] += g1[...]
    push(("G2",), gwp.at[c, 1 - xl], g2, across)
    ring_q(3)
    chip_sum(2)
    chip_sum(-2)
    ring_p(3)
    take(("G2",))
    r3[z] = gwp[c, xl] + g2[...]
    for k in range(1, NZ):
        push(("G3", k), r3.at[z], r3.at[z], dev(z_=zz(k)))
    ring_q(2)
    chip_sum(1)
    chip_sum(-1)
    chip_sum(0)
    ring_p(2)
    for k in range(1, NZ):
        take(("G3", k))
    fin = r3[0]
    for k in range(1, NZ):
        fin = fin + r3[k]
    gb_out[:, pl.ds(0, 128)] = fin[0:1, 256:]
    gb_out[:, pl.ds(128, 128)] = fin[1:2, 256:]
    gwo[y, xh, xl, c] = fin[:, :256]
    for k in range(1, NY):
        ref = gwo.at[y, xh, xl, c]
        push(("G4", k), ref, ref, dev(y_=yy(k)))
    ring_q(1)
    for k in range(1, NY):
        take(("G4", k))
    for i, (a, b) in enumerate(((0, 1), (1, 0), (1, 1))):
        ref = gwo.at[:, xh, xl, c]
        push(("G5", i), ref, ref, dev(xh_=(1 - xh) if a else xh, xl_=(1 - xl) if b else xl))
    ring_p(1)

    col = col_of(0, True)
    for d in both:
        take(("RQ", d, 1))
    g_own[col, q_rows] += lq[0, 0] + lq[1, 0]
    push(("XF",), g_own.at[col, q_rows], xq, across)
    for i in range(3):
        take(("G5", i))
    ref = gwo.at[:, :, :, c]
    push(("G6",), ref, ref, twin)
    col = col_of(0, False)
    for d in both:
        take(("REQ", d, 1))
    take(("RX", 0))
    for d in both:
        take(("REP", d, 1))
    take(("XF",))
    g_own[col, q_rows] += le[0, 0, q_rows] + le[1, 0, q_rows] + xq[...]
    g_own[col, p_rows] += le[0, 0, p_rows] + le[1, 0, p_rows] + rx[slot_of[0]]
    gf_out[...] = g_own[col].T
    take(("G6",))
    gw_out[...] = gwo[...].reshape(256, 256)

    for store in stores:
        store.wait()
    for copy in msgs.values():
        copy.wait_send()


def deliver(hid, gf, gw, gb, hid_out, gf_out, gw_out, gb_out, hid_v, gf_v, gw_v, gb_v, sem_in, sem_out):
    steps = [(hid.at[pl.ds(i * T, T)], hid_v.at[pl.ds(i * T, T)], hid_out.at[pl.ds(i * T, T)]) for i in range(4)]
    steps += [(gf, gf_v, gf_out), (gw, gw_v, gw_out), (gb, gb_v, gb_out)]
    ins = [pltpu.make_async_copy(a, v, sem_in.at[i]) for i, (a, v, _) in enumerate(steps)]
    outs = [pltpu.make_async_copy(v, o, sem_out.at[i]) for i, (_, v, o) in enumerate(steps)]
    for copy in ins:
        copy.start()
    for first, then in zip(ins, outs):
        first.wait()
        then.start()
    for copy in outs:
        copy.wait()


def on_device(features, tiles, cols, counts, weight, bias, cot):
    n_rows = cot.shape[0]
    scaling = 1.0 / float(n_rows * 32) ** 0.5
    vmem = pl.BlockSpec(memory_space=pltpu.VMEM)
    hbm = pl.BlockSpec(memory_space=pl.ANY)
    shape = jax.ShapeDtypeStruct
    V = pltpu.VMEM
    scratch = [
        V((32, 128, 128), F32), V((32, 128, 128), F32),
        V((4, 6, T, T), F32),
        V((4, T, 6 * T), BF16), V((4, T, 6 * T), BF16),
        V((6 * T, 128), BF16), V((6 * T, 128), BF16),
        V((T, T), F32), V((T, T), BF16), V((T, T), BF16),
        V((1, T), F32),
        V((1024, T), F32),
        V((2, 1024, 128), F32),
        V((2, 4, 2, 32, 128), F32), V((2, 4, 2, 64, 128), F32),
        V((2, 4, 64, 128), F32), V((2, 4, 64, 128), F32),
        V((2, 1024, 128), F32), V((1024, T), F32),
        V((T, T), F32), V((1, T), F32),
        V((24, 2, T, 128), F32),
        V((16, T, 128), F32), V((16, T, 128), F32), V((16, T, 128), F32),
        V((8, T - RS_Q, 128), F32),
        V((2, 4, T, 128), F32), V((2, 4, RS_Q, 128), F32),
        V((RS_Q, 128), F32),
        V((2, 2, 8, 384), F32), V((2, 8, 384), F32), V((8, 384), F32),
        V((8, 8, 384), F32),
        V((4, 2, 2, 2, 8, T), F32),
        pltpu.SMEM((4, 1, 6), jnp.int32), pltpu.SMEM((1, 4), jnp.int32),
        pltpu.SMEM((64,), jnp.int32), pltpu.SMEM((64,), F32),
        pltpu.SemaphoreType.DMA((N_MSG,)), pltpu.SemaphoreType.DMA((N_MSG,)),
        pltpu.SemaphoreType.DMA((24,)),
    ]
    outs = (shape((1024, T), F32), shape((128, T), F32), shape((T, T), F32), shape((1, T), F32))
    results = pl.pallas_call(
        functools.partial(kernel, scaling),
        out_shape=outs,
        in_specs=[hbm] * 7,
        out_specs=(hbm, vmem, vmem, vmem),
        scratch_shapes=scratch,
        compiler_params=pltpu.CompilerParams(
            collective_id=0, has_side_effects=True, vmem_limit_bytes=60 << 20,
        ),
        name="graph_layer",
    )(features, tiles, cols, counts.T, weight, bias.reshape(1, T), cot)
    hid, gf, gw, gb = pl.pallas_call(
        deliver,
        out_shape=outs,
        in_specs=[hbm] * 4,
        out_specs=(hbm,) * 4,
        scratch_shapes=[V(o.shape, F32) for o in outs] + [pltpu.SemaphoreType.DMA((7,))] * 2,
        name="deliver",
    )(*results)
    return hid, gf, gw, gb.reshape(T)


def solution(mesh):
    return jax.shard_map(
        on_device,
        mesh=mesh,
        in_specs=(
            P(("grp", "row"), None),
            P("row", "grp", None, None, None),
            P("row", "grp", None),
            P("row", "grp"),
            P(),
            P(),
            P("row", None),
        ),
        out_specs=(P("row", None), P(("grp", "row"), None), P(), P()),
        check_vma=False,
    )
```

```python
import functools

import jax
import jax.numpy as jnp
from jax import lax
from jax.experimental import pallas as pl
from jax.experimental.pallas import tpu as pltpu
from jax.sharding import PartitionSpec as P

MESH = pl.DeviceIdType.MESH
F32, BF16 = jnp.float32, jnp.bfloat16
NZ, NY = 8, 4
T = 256
AG_Q = 56
RS_Q = 112
N_MSG, N_SEND = 119, 48


def split(x):
    hi = x.astype(BF16)
    return hi, (x - hi.astype(F32)).astype(BF16)


def dot(a, b, ca=1, cb=0):
    return lax.dot_general(a, b, (((ca,), (cb,)), ((), ())), preferred_element_type=F32)


def dot3(a, b, ca=1, cb=0):
    (ah, al), (bh, bl) = a, b
    return dot(ah, bh, ca, cb) + dot(ah, bl, ca, cb) + dot(al, bh, ca, cb)


def kernel(
    scaling,
    feat, tiles, cols_in, counts_in, weight, bias_in, cot,
    hid_out, gf_out, gw_out, gb_out,
    panel_a, panel_b, stage, a_hi, a_lo, x_hi, x_lo, w_v, w_hi, w_lo, bias, cot_v,
    part, y1, y2, ysum, arx, agg, hid, gw_acc, gb_acc,
    spread, g_send, g_own, g_recv, rx, le, lq, xq,
    gwp, g1, g2, r3, gwo, cols, counts, inv, msk,
    send_sem, recv_sem, load_sem,
):
    row, grp = lax.axis_index("row"), lax.axis_index("grp")
    z, xl, c = lax.div(row, 4), lax.rem(lax.div(row, 2), 2), lax.rem(row, 2)
    y, xh = lax.div(grp, 2), lax.rem(grp, 2)

    def zz(k):
        return lax.rem(z + (k + NZ), NZ)

    def yy(k):
        return lax.rem(y + (k + NY), NY)

    def dev(z_=None, xl_=None, c_=None, y_=None, xh_=None):
        z_, xl_, c_ = z if z_ is None else z_, xl if xl_ is None else xl_, c if c_ is None else c_
        y_, xh_ = y if y_ is None else y_, xh if xh_ is None else xh_
        return {"grp": y_ * 2 + xh_, "row": z_ * 4 + xl_ * 2 + c_}

    def blk(z_, xl_, c_):
        return z_ * 4 + xl_ * 2 + c_

    def m8(v):
        return pl.multiple_of(v, 8)

    panels = (panel_a, panel_b)
    sends, groups = [], {}

    def push(group, src, dst, device):
        at, slot = groups.setdefault(group, len(groups)), len(sends) % N_SEND
        if len(sends) >= N_SEND:
            sends[-N_SEND].wait_send()
        copy = pltpu.make_async_remote_copy(
            src_ref=src, dst_ref=dst, send_sem=send_sem.at[slot], recv_sem=recv_sem.at[at],
            device_id=device, device_id_type=MESH,
        )
        copy.start()
        sends.append(copy)

    def take(group, ref):
        pltpu.make_async_copy(ref, ref, recv_sem.at[groups[group]]).wait()

    own = blk(z, xl, c)
    n_loads = [0]

    def load(src, dst):
        copy = pltpu.make_async_copy(src, dst, load_sem.at[n_loads[0]])
        copy.start()
        n_loads[0] += 1
        return copy

    barrier = pltpu.get_barrier_semaphore()
    peers = [dev(z_=zz(k)) for k in range(1, NZ)] + [dev(y_=yy(k)) for k in range(1, NY)]
    peers += [dev(xl_=1 - xl), dev(xh_=1 - xh), dev(xl_=1 - xl, xh_=1 - xh), dev(c_=1 - c)]
    for peer in peers:
        pl.semaphore_signal(barrier, inc=1, device_id=peer, device_id_type=MESH)

    feat_loads = [load(feat.at[:, pl.ds(h * 128, 128)], panels[h].at[own]) for h in range(2)]
    small_loads = [load(cols_in, cols), load(counts_in, counts), load(weight, w_v), load(bias_in, bias)]
    tile_loads = [load(tiles.at[b, 0], stage.at[b]) for b in range(4)]
    cot_load = load(cot, cot_v)
    for copy in feat_loads:
        copy.wait()
    pl.semaphore_wait(barrier, len(peers))

    up, down, across, twin = dev(z_=zz(1)), dev(z_=zz(-1)), dev(xl_=1 - xl), dev(c_=1 - c)
    along = {1: up, -1: down}
    both = (1, -1)
    AG_P = 128 - AG_Q
    ep_half = {1: (AG_Q, 40), -1: (AG_Q + 40, AG_P - 40)}
    eq_half = {1: (0, 32), -1: (32, AG_Q - 32)}

    def same(h, key, at, span, device):
        ref = panels[h].at[at, pl.ds(*span)]
        push((h, *key), ref, ref, device)

    def took(h, key, blocks, count):
        take((h, *key), panels[h].at[pl.ds(0, blocks), pl.ds(0, count)])

    def ag_init(h):
        same(h, ("Q", 0), own, (0, AG_Q), across)
        for d in both:
            same(h, ("EP", 1), own, (AG_Q, AG_P), along[d])
        for d in both:
            same(h, ("EQ", 1), own, (0, AG_Q), along[d])
        same(h, ("P", 0), own, (AG_Q, AG_P), across)
        same(h, ("SS",), own, (0, 128), twin)

    def ag_crossed(h, o):
        took(h, ("P", o), 1, AG_P)
        same(h, ("SS",), blk(zz(-o), 1 - xl, c), (0, 128), twin)

    def ag_e(h, k):
        took(h, ("EP", k), 2, AG_P)
        for d in both:
            at = blk(zz(-d * k), xl, c)
            same(h, ("EP", k + 1), at, (AG_Q, AG_P) if k < 3 else ep_half[d], along[d])
        for d in both:
            same(h, ("P", d * k), blk(zz(-d * k), xl, c), (AG_Q, AG_P), across)
        took(h, ("EQ", k), 2, AG_Q)
        for d in both:
            at = blk(zz(-d * k), xl, c)
            same(h, ("EQ", k + 1), at, (0, AG_Q) if k < 3 else eq_half[d], along[d])
        for d in both:
            same(h, ("SS",), blk(zz(-d * k), xl, c), (0, 128), twin)

    def ag_q(h, k):
        took(h, ("Q", k), 1 if k == 0 else 2, AG_Q)
        for d in both:
            at = blk(zz(-d * k), 1 - xl, c)
            same(h, ("Q", k + 1), at, (0, AG_Q) if k < 3 else eq_half[d], along[d])

    def ag_step(h, k):
        if k < 4:
            ag_e(h, k)
        else:
            at = blk(zz(4), xl, c)
            took(h, ("EP", 4), 1, AG_P)
            same(h, ("P", 4), at, (AG_Q, AG_P), across)
            took(h, ("EQ", 4), 1, AG_Q)
            same(h, ("SS",), at, (0, 128), twin)
        ag_q(h, k - 1)
        for o in {1: (), 2: (0,), 3: (1, -1), 4: (2, -2)}[k]:
            ag_crossed(h, o)

    def ag_end(h):
        took(h, ("Q", 4), 1, AG_Q)
        ag_crossed(h, 3)
        ag_crossed(h, -3)
        ag_crossed(h, 4)
        took(h, ("SS",), 16, 128)

    def prepare_tables():
        for copy in small_loads:
            copy.wait()
        wh, wl = split(w_v[...])
        w_hi[...] = wh
        w_lo[...] = wl

        @pl.loop(0, 64)
        def _(i):
            b, col = lax.div(i, 16), lax.rem(i, 16)
            slot, live = jnp.int32(0), jnp.float32(0)
            for t in range(6):
                hit = jnp.logical_and(cols[b, 0, t] == col, counts[0, b] > t)
                slot = jnp.where(hit, b * 6 + t, slot)
                live = jnp.where(hit, jnp.float32(1), live)
            inv[i] = slot
            msk[i] = live

    def prepare(b):
        tile_loads[b].wait()
        for t in range(6):
            hi, lo = split(stage[b, t])
            a_hi[b, :, pl.ds(t * T, T)] = hi
            a_lo[b, :, pl.ds(t * T, T)] = lo

    def forward(h, b):
        for t in range(6):
            at = cols[b, 0, t]
            live = jnp.where(counts[0, b] > t, jnp.float32(1), jnp.float32(0))
            hi, lo = split(panels[h][pl.ds(2 * at, 2)].reshape(T, 128) * live)
            x_hi[pl.ds(t * T, T), :] = hi
            x_lo[pl.ds(t * T, T), :] = lo
        part[h, pl.ds(b * T, T), :] = dot3((a_hi[b], a_lo[b]), (x_hi[...], x_lo[...]))

    ahead, behind, opposite = dev(y_=yy(1)), dev(y_=yy(-1)), dev(xh_=1 - xh)

    def rows(b, k, first, count):
        return pl.ds(m8(b * T + yy(k) * 64 + first), count)

    def s1(h, b):
        forward(h, b)
        push((h, "Y1", b), part.at[h, rows(b, 2, 0, 32)], y1.at[h, b, 0], ahead)
        push((h, "Y1", b), part.at[h, rows(b, 2, 32, 32)], y1.at[h, b, 1], behind)

    def s2(h, b):
        take((h, "Y1", b), y1.at[h, b])
        part[h, rows(b, 1, 0, 32)] += y1[h, b, 0]
        part[h, rows(b, -1, 32, 32)] += y1[h, b, 1]
        push((h, "Y2", b), part.at[h, rows(b, 1, 0, 64)], y2.at[h, b, 0], ahead)
        push((h, "Y2", b), part.at[h, rows(b, -1, 0, 64)], y2.at[h, b, 1], behind)

    def s3(h, b):
        take((h, "Y2", b), y2.at[h, b])
        ysum[h, b] = part[h, rows(b, 0, 0, 64)] + y2[h, b, 0] + y2[h, b, 1]
        push((h, "X", b), ysum.at[h, b], arx.at[h, b], opposite)

    def s4(h, b):
        take((h, "X", b), arx.at[h, b])
        agg[h, rows(b, 0, 0, 64)] = ysum[h, b] + arx[h, b]
        mine = agg.at[h, rows(b, 0, 0, 64)]
        push((h, "Y3", b), mine, mine, ahead)
        push((h, "Y3", b), mine, mine, behind)

    def s5(h, b):
        take((h, "Y3", b), agg.at[h, pl.ds(0, 128)])
        ref = agg.at[h, rows(b, -1, 0, 32)]
        push((h, "Y4", b), ref, ref, ahead)
        ref = agg.at[h, rows(b, 1, 32, 32)]
        push((h, "Y4", b), ref, ref, behind)

    def s6(h, b):
        take((h, "Y4", b), agg.at[h, pl.ds(0, 64)])

    stores = []

    def dense(b):
        span = pl.ds(b * T, T)
        summed = jnp.concatenate([agg[0, span], agg[1, span]], axis=1)
        w = (w_hi[...], w_lo[...])
        pre = dot3(split(summed), w) + bias[...]
        sigma = jax.nn.sigmoid(pre)
        hid[span, :] = pre * sigma
        stores.append(load(hid.at[span], hid_out.at[span]))
        grad = cot_v[span, :] * sigma * (1.0 + pre * (1.0 - sigma))
        gs = split(grad)
        bh, bl = split(dot3(w, gs, 1, 1))
        for t in range(6):
            tile = pl.ds(t * T, T)
            sp = dot3((bh, bl), (a_hi[b, :, tile], a_lo[b, :, tile]))
            spread[b * 6 + t, 0] = sp[:, :128]
            spread[b * 6 + t, 1] = sp[:, 128:]
        gw = dot3(split(summed.T), gs)
        gb = jnp.sum(grad, axis=0, keepdims=True)
        gw_acc[...] = gw if b == 0 else gw_acc[...] + gw
        gb_acc[...] = gb if b == 0 else gb_acc[...] + gb

    ag_init(0)
    prepare_tables()
    ag_step(0, 1)
    ag_init(1)
    prepare(0)
    ag_step(0, 2)
    ag_step(1, 1)
    prepare(1)
    ag_step(0, 3)
    ag_step(1, 2)
    prepare(2)
    ag_step(0, 4)
    ag_step(1, 3)
    prepare(3)
    ag_end(0)
    s1(0, 0)
    s1(0, 1)
    ag_step(1, 4)
    s1(0, 2)
    s1(0, 3)
    for b in range(4):
        s2(0, b)
    ag_end(1)
    s1(1, 0)
    s3(0, 0)
    s3(0, 1)
    s1(1, 1)
    s3(0, 2)
    s3(0, 3)
    s1(1, 2)
    s1(1, 3)
    s2(1, 0)
    s4(0, 0)
    s2(1, 1)
    s4(0, 1)
    s2(1, 2)
    s4(0, 2)
    s2(1, 3)
    s4(0, 3)
    for b in range(4):
        s3(1, b)
        s5(0, b)
    for b in range(4):
        s4(1, b)
    cot_load.wait()
    for b in range(4):
        s6(0, b)
        s5(1, b)
        if b > 0:
            s6(1, b - 1)
            dense(b - 1)
    s6(1, 3)
    dense(3)

    gwp[...] = jnp.zeros_like(gwp)
    for c_ in range(2):
        for xl_ in range(2):
            piece = gw_acc[pl.ds(m8(grp * 32 + (xl_ * 2 + c_) * 8), 8), :]
            gwp[c_, xl_, :, pl.ds(0, 256)] = piece * scaling
            gwp[c_, xl_, pl.ds(0, 1), pl.ds(256, 128)] = gb_acc[:, pl.ds(0, 128)] * scaling
            gwp[c_, xl_, pl.ds(1, 1), pl.ds(256, 128)] = gb_acc[:, pl.ds(128, 128)] * scaling
    push("G1", gwp.at[1 - c], g1, twin)

    def g_step(i):
        if i == 1:
            take("G1", g1)
            gwp[c] += g1[...]
            push("G2", gwp.at[c, 1 - xl], g2, across)
        elif i == 2:
            take("G2", g2)
            r3[z] = gwp[c, xl] + g2[...]
            for k in range(1, NZ):
                push("G3", r3.at[z], r3.at[z], dev(z_=zz(k)))
        elif i == 3:
            take("G3", r3.at[pl.ds(0, NZ - 1)])
            fin = r3[0]
            for k in range(1, NZ):
                fin = fin + r3[k]
            gb_out[:, pl.ds(0, 128)] = fin[0:1, 256:]
            gb_out[:, pl.ds(128, 128)] = fin[1:2, 256:]
            gwo[y, xh, xl, c] = fin[:, :256]
            for k in range(1, NY):
                ref = gwo.at[y, xh, xl, c]
                push("G4", ref, ref, dev(y_=yy(k)))
        elif i == 4:
            take("G4", gwo.at[pl.ds(0, NY - 1), 0, 0, 0])
            ref = gwo.at[:, xh, xl, c]
            for a, b in ((0, 1), (1, 0), (1, 1)):
                push("G5", ref, ref, dev(xh_=(1 - xh) if a else xh, xl_=(1 - xl) if b else xl))
        elif i == 5:
            take("G5", gwo.at[pl.ds(0, 3), :, :, 0])
            ref = gwo.at[:, :, :, c]
            push("G6", ref, ref, twin)

    def gather(col, half):
        total = None
        for b in range(4):
            at = b * 16 + col
            term = spread[inv[at], half] * msk[at]
            total = term if total is None else total + term
        return total

    slot_of = {o: i for i, o in enumerate((4, 3, -3, 2, -2, 1, -1, 0))}
    lane_of = {1: 0, -1: 1}
    RS_P = T - RS_Q
    p_rows, q_rows = pl.ds(RS_Q, RS_P), pl.ds(0, RS_Q)

    def col_of(o, other):
        return zz(o) * 2 + ((1 - xl) if other else xl)

    def pair_of(o):
        return pl.ds(pl.multiple_of(zz(o) * 2, 2), 2)

    def to_twin(o):
        for other in (True, False):
            col = col_of(o, other)
            g_send[col] = gather(col, 1 - c)
        push(("S", o), g_send.at[pair_of(o)], g_recv.at[pair_of(o)], twin)

    def chip_sum(o):
        take(("S", o), g_recv.at[pair_of(o)])
        for other in (True, False):
            col = col_of(o, other)
            g_own[col] = gather(col, c) + g_recv[col]
            if other:
                push(("RX", o), g_own.at[col, p_rows], rx.at[slot_of[o]], across)

    q_part = {1: pl.ds(0, 56), -1: pl.ds(56, 56)}
    p_part = {1: pl.ds(RS_Q, 72), -1: pl.ds(RS_Q + 72, 72)}

    def ring_q(k):
        for other, name, land in ((True, "RQ", lq), (False, "REQ", le)):
            if k < 4:
                take((name, k + 1), land.at[0, 0, q_rows] if k == 3 else land.at[:, 0, q_rows])
            for d in both:
                col = col_of(d * k, other)
                if k < 4:
                    got = q_part[d] if k == 3 else q_rows
                    g_own[col, got] += land[lane_of[d], k, got]
                span = q_part[d] if k == 4 else q_rows
                push((name, k), g_own.at[col, span], land.at[lane_of[d], k - 1, span], along[d])

    def ring_p(k):
        for o in ((4,) if k == 4 else (k, -k)):
            take(("RX", o), rx.at[slot_of[o]])
            g_own[col_of(o, False), p_rows] += rx[slot_of[o]]
        if k < 4:
            take(("REP", k + 1), le.at[0, 0, p_rows] if k == 3 else le.at[:, 0, p_rows])
        for d in both:
            col = col_of(d * k, False)
            if k < 4:
                got = p_part[d] if k == 3 else p_rows
                g_own[col, got] += le[lane_of[d], k, got]
            span = p_part[d] if k == 4 else p_rows
            push(("REP", k), g_own.at[col, span], le.at[lane_of[d], k - 1, span], along[d])

    to_twin(4)
    to_twin(3)
    to_twin(-3)
    chip_sum(4)
    ring_q(4)
    chip_sum(3)
    chip_sum(-3)
    g_step(1)
    to_twin(2)
    to_twin(-2)
    to_twin(1)
    to_twin(-1)
    to_twin(0)
    chip_sum(2)
    chip_sum(-2)
    ring_q(3)
    ring_p(4)
    chip_sum(1)
    chip_sum(-1)
    chip_sum(0)
    g_step(2)
    ring_q(2)
    ring_p(3)
    ring_q(1)
    ring_p(2)
    g_step(3)

    far, near = col_of(0, True), col_of(0, False)
    take(("RQ", 1), lq.at[:, 0])
    g_own[far, q_rows] += lq[0, 0] + lq[1, 0]
    push("XF", g_own.at[far, q_rows], xq, across)
    ring_p(1)
    g_step(4)
    take(("RX", 0), rx.at[slot_of[0]])
    take(("REQ", 1), le.at[:, 0, q_rows])
    take("XF", xq)
    g_own[near, q_rows] += le[0, 0, q_rows] + le[1, 0, q_rows] + xq[...]
    g_step(5)
    take(("REP", 1), le.at[:, 0, p_rows])
    g_own[near, p_rows] += le[0, 0, p_rows] + le[1, 0, p_rows] + rx[slot_of[0]]
    gf_out[...] = g_own[near].T
    take("G6", gwo.at[:, :, :, 0])
    gw_out[...] = gwo[...].reshape(256, 256)

    assert len(groups) == N_MSG and n_loads[0] == 15
    for store in stores:
        store.wait()
    for copy in sends[-N_SEND:]:
        copy.wait_send()


def deliver(hid, gf, gw, gb, hid_out, gf_out, gw_out, gb_out, hid_v, gf_v, gw_v, gb_v, sem_in, sem_out):
    steps = [(hid.at[pl.ds(i * T, T)], hid_v.at[pl.ds(i * T, T)], hid_out.at[pl.ds(i * T, T)]) for i in range(4)]
    steps += [(gf, gf_v, gf_out), (gw, gw_v, gw_out), (gb, gb_v, gb_out)]
    ins = [pltpu.make_async_copy(a, v, sem_in.at[i]) for i, (a, v, _) in enumerate(steps)]
    outs = [pltpu.make_async_copy(v, o, sem_out.at[i]) for i, (_, v, o) in enumerate(steps)]
    for copy in ins:
        copy.start()
    for first, then in zip(ins, outs):
        first.wait()
        then.start()
    for copy in outs:
        copy.wait()


def on_device(features, tiles, cols, counts, weight, bias, cot):
    n_rows = cot.shape[0]
    scaling = 1.0 / float(n_rows * 32) ** 0.5
    vmem = pl.BlockSpec(memory_space=pltpu.VMEM)
    hbm = pl.BlockSpec(memory_space=pl.ANY)
    shape = jax.ShapeDtypeStruct
    V = pltpu.VMEM
    scratch = [
        V((32, 128, 128), F32), V((32, 128, 128), F32),
        V((4, 6, T, T), F32),
        V((4, T, 6 * T), BF16), V((4, T, 6 * T), BF16),
        V((6 * T, 128), BF16), V((6 * T, 128), BF16),
        V((T, T), F32), V((T, T), BF16), V((T, T), BF16),
        V((1, T), F32),
        V((1024, T), F32),
        V((2, 1024, 128), F32),
        V((2, 4, 2, 32, 128), F32), V((2, 4, 2, 64, 128), F32),
        V((2, 4, 64, 128), F32), V((2, 4, 64, 128), F32),
        V((2, 1024, 128), F32), V((1024, T), F32),
        V((T, T), F32), V((1, T), F32),
        V((24, 2, T, 128), F32),
        V((16, T, 128), F32), V((16, T, 128), F32), V((16, T, 128), F32),
        V((8, T - RS_Q, 128), F32),
        V((2, 4, T, 128), F32), V((2, 4, RS_Q, 128), F32),
        V((RS_Q, 128), F32),
        V((2, 2, 8, 384), F32), V((2, 8, 384), F32), V((8, 384), F32),
        V((8, 8, 384), F32),
        V((4, 2, 2, 2, 8, T), F32),
        pltpu.SMEM((4, 1, 6), jnp.int32), pltpu.SMEM((1, 4), jnp.int32),
        pltpu.SMEM((64,), jnp.int32), pltpu.SMEM((64,), F32),
        pltpu.SemaphoreType.DMA((N_SEND,)), pltpu.SemaphoreType.DMA((N_MSG,)),
        pltpu.SemaphoreType.DMA((15,)),
    ]
    outs = (shape((1024, T), F32), shape((128, T), F32), shape((T, T), F32), shape((1, T), F32))
    results = pl.pallas_call(
        functools.partial(kernel, scaling),
        out_shape=outs,
        in_specs=[hbm] * 7,
        out_specs=(hbm, vmem, vmem, vmem),
        scratch_shapes=scratch,
        compiler_params=pltpu.CompilerParams(
            collective_id=0, has_side_effects=True, vmem_limit_bytes=60 << 20,
        ),
        name="graph_layer",
    )(features, tiles, cols, counts.T, weight, bias.reshape(1, T), cot)
    hid, gf, gw, gb = pl.pallas_call(
        deliver,
        out_shape=outs,
        in_specs=[hbm] * 4,
        out_specs=(hbm,) * 4,
        scratch_shapes=[V(o.shape, F32) for o in outs] + [pltpu.SemaphoreType.DMA((7,))] * 2,
        name="deliver",
    )(*results)
    return hid, gf, gw, gb.reshape(T)


def solution(mesh):
    return jax.shard_map(
        on_device,
        mesh=mesh,
        in_specs=(
            P(("grp", "row"), None),
            P("row", "grp", None, None, None),
            P("row", "grp", None),
            P("row", "grp"),
            P(),
            P(),
            P("row", None),
        ),
        out_specs=(P("row", None), P(("grp", "row"), None), P(), P()),
        check_vma=False,
    )
```

```python
import functools

import jax
import jax.numpy as jnp
from jax import lax
from jax.experimental import pallas as pl
from jax.experimental.pallas import tpu as pltpu
from jax.sharding import PartitionSpec as P

MESH = pl.DeviceIdType.MESH
F32, BF16 = jnp.float32, jnp.bfloat16
NZ, NY = 8, 4
T = 256
AG_Q = 56
RS_Q = 112
N_MSG, N_SEND = 188, 48


def split(x):
    hi = x.astype(BF16)
    return hi, (x - hi.astype(F32)).astype(BF16)


def dot(a, b, ca=1, cb=0):
    return lax.dot_general(a, b, (((ca,), (cb,)), ((), ())), preferred_element_type=F32)


def dot3(a, b, ca=1, cb=0):
    (ah, al), (bh, bl) = a, b
    return dot(ah, bh, ca, cb) + dot(ah, bl, ca, cb) + dot(al, bh, ca, cb)


def kernel(
    scaling,
    feat, tiles, cols_in, counts_in, weight, bias_in, cot,
    hid_out, gf_out, gw_out, gb_out,
    panel_a, panel_b, stage, a_hi, a_lo, x_hi, x_lo, w_v, w_hi, w_lo, bias, cot_v,
    part, y1, y2, ysum, arx, agg, hid, gw_acc, gb_acc,
    spread, g_send, g_own, g_recv, rx, le, lq, xq,
    gwp, g1, g2, r3, gwo, cols, counts, inv, msk,
    send_sem, recv_sem, load_sem,
):
    row, grp = lax.axis_index("row"), lax.axis_index("grp")
    z, xl, c = lax.div(row, 4), lax.rem(lax.div(row, 2), 2), lax.rem(row, 2)
    y, xh = lax.div(grp, 2), lax.rem(grp, 2)

    def zz(k):
        return lax.rem(z + (k + NZ), NZ)

    def yy(k):
        return lax.rem(y + (k + NY), NY)

    def dev(z_=None, xl_=None, c_=None, y_=None, xh_=None):
        z_, xl_, c_ = z if z_ is None else z_, xl if xl_ is None else xl_, c if c_ is None else c_
        y_, xh_ = y if y_ is None else y_, xh if xh_ is None else xh_
        return {"grp": y_ * 2 + xh_, "row": z_ * 4 + xl_ * 2 + c_}

    def blk(z_, xl_, c_):
        return z_ * 4 + xl_ * 2 + c_

    def m8(v):
        return pl.multiple_of(v, 8)

    panels = (panel_a, panel_b)
    sends, groups = [], {}

    def push(group, src, dst, device):
        at, slot = groups.setdefault(group, len(groups)), len(sends) % N_SEND
        if len(sends) >= N_SEND:
            sends[-N_SEND].wait_send()
        copy = pltpu.make_async_remote_copy(
            src_ref=src, dst_ref=dst, send_sem=send_sem.at[slot], recv_sem=recv_sem.at[at],
            device_id=device, device_id_type=MESH,
        )
        copy.start()
        sends.append(copy)

    def take(group, ref):
        pltpu.make_async_copy(ref, ref, recv_sem.at[groups[group]]).wait()

    own = blk(z, xl, c)
    n_loads = [0]

    def load(src, dst):
        copy = pltpu.make_async_copy(src, dst, load_sem.at[n_loads[0]])
        copy.start()
        n_loads[0] += 1
        return copy

    barrier = pltpu.get_barrier_semaphore()
    plane = [
        dev(y_=yy(i // 4), xh_=(1 - xh) if i // 2 % 2 else xh, xl_=(1 - xl) if i % 2 else xl)
        for i in range(1, 16)
    ]
    peers = [dev(z_=zz(k)) for k in range(1, NZ)] + plane + [dev(c_=1 - c)]
    for peer in peers:
        pl.semaphore_signal(barrier, inc=1, device_id=peer, device_id_type=MESH)

    feat_loads = [load(feat.at[:, pl.ds(h * 128, 128)], panels[h].at[own]) for h in range(2)]
    small_loads = [load(cols_in, cols), load(counts_in, counts), load(weight, w_v), load(bias_in, bias)]
    tile_loads = [load(tiles.at[b, 0], stage.at[b]) for b in range(4)]
    cot_load = load(cot, cot_v)
    for copy in feat_loads:
        copy.wait()
    pl.semaphore_wait(barrier, len(peers))

    up, down, across, twin = dev(z_=zz(1)), dev(z_=zz(-1)), dev(xl_=1 - xl), dev(c_=1 - c)
    along = {1: up, -1: down}
    both = (1, -1)
    AG_P = 128 - AG_Q
    ep_half = {1: (AG_Q, 40), -1: (AG_Q + 40, AG_P - 40)}
    eq_half = {1: (0, 32), -1: (32, AG_Q - 32)}

    def same(h, key, at, span, device):
        ref = panels[h].at[at, pl.ds(*span)]
        push((h, *key), ref, ref, device)

    def took(h, key, blocks, count):
        take((h, *key), panels[h].at[pl.ds(0, blocks), pl.ds(0, count)])

    def ag_init(h):
        same(h, ("Q", 0), own, (0, AG_Q), across)
        for d in both:
            same(h, ("EP", d, 1), own, (AG_Q, AG_P), along[d])
        for d in both:
            same(h, ("EQ", d, 1), own, (0, AG_Q), along[d])
        same(h, ("P", 0), own, (AG_Q, AG_P), across)
        same(h, ("SS",), own, (0, 128), twin)

    def ag_crossed(h, o):
        took(h, ("P", o), 1, AG_P)
        same(h, ("SS",), blk(zz(-o), 1 - xl, c), (0, 128), twin)

    def ag_e(h, k):
        for d in both:
            at = blk(zz(-d * k), xl, c)
            took(h, ("EP", d, k), 1, AG_P)
            same(h, ("EP", d, k + 1), at, (AG_Q, AG_P) if k < 3 else ep_half[d], along[d])
            same(h, ("P", d * k), at, (AG_Q, AG_P), across)
        for d in both:
            at = blk(zz(-d * k), xl, c)
            took(h, ("EQ", d, k), 1, AG_Q)
            same(h, ("EQ", d, k + 1), at, (0, AG_Q) if k < 3 else eq_half[d], along[d])
            same(h, ("SS",), at, (0, 128), twin)

    def ag_q(h, k):
        if k == 0:
            took(h, ("Q", 0), 1, AG_Q)
        for d in both:
            at = blk(zz(-d * k), 1 - xl, c)
            if k > 0:
                took(h, ("Q", d, k), 1, AG_Q)
            same(h, ("Q", d, k + 1), at, (0, AG_Q) if k < 3 else eq_half[d], along[d])

    def ag_step(h, k):
        if k < 4:
            ag_e(h, k)
        else:
            at = blk(zz(4), xl, c)
            for d in both:
                took(h, ("EP", d, 4), 1, ep_half[d][1])
            same(h, ("P", 4), at, (AG_Q, AG_P), across)
            for d in both:
                took(h, ("EQ", d, 4), 1, eq_half[d][1])
            same(h, ("SS",), at, (0, 128), twin)
        ag_q(h, k - 1)
        for o in {1: (), 2: (0,), 3: (1, -1), 4: (2, -2)}[k]:
            ag_crossed(h, o)

    def ag_end(h):
        ag_crossed(h, 3)
        ag_crossed(h, -3)
        for d in both:
            took(h, ("Q", d, 4), 1, eq_half[d][1])
        ag_crossed(h, 4)
        took(h, ("SS",), 16, 128)

    def prepare_tables():
        for copy in small_loads:
            copy.wait()
        wh, wl = split(w_v[...])
        w_hi[...] = wh
        w_lo[...] = wl

        @pl.loop(0, 64)
        def _(i):
            b, col = lax.div(i, 16), lax.rem(i, 16)
            slot, live = jnp.int32(0), jnp.float32(0)
            for t in range(6):
                hit = jnp.logical_and(cols[b, 0, t] == col, counts[0, b] > t)
                slot = jnp.where(hit, b * 6 + t, slot)
                live = jnp.where(hit, jnp.float32(1), live)
            inv[i] = slot
            msk[i] = live

    def prepare(b):
        tile_loads[b].wait()
        for t in range(6):
            hi, lo = split(stage[b, t])
            a_hi[b, :, pl.ds(t * T, T)] = hi
            a_lo[b, :, pl.ds(t * T, T)] = lo

    def forward(h, b):
        for t in range(6):
            at = cols[b, 0, t]
            live = jnp.where(counts[0, b] > t, jnp.float32(1), jnp.float32(0))
            hi, lo = split(panels[h][pl.ds(2 * at, 2)].reshape(T, 128) * live)
            x_hi[pl.ds(t * T, T), :] = hi
            x_lo[pl.ds(t * T, T), :] = lo
        part[h, pl.ds(b * T, T), :] = dot3((a_hi[b], a_lo[b]), (x_hi[...], x_lo[...]))

    ahead, behind, opposite = dev(y_=yy(1)), dev(y_=yy(-1)), dev(xh_=1 - xh)

    def rows(b, k, first, count):
        return pl.ds(m8(b * T + yy(k) * 64 + first), count)

    def s1(h, b):
        forward(h, b)
        push((h, "Y1", 1, b), part.at[h, rows(b, 2, 0, 32)], y1.at[h, b, 0], ahead)
        push((h, "Y1", -1, b), part.at[h, rows(b, 2, 32, 32)], y1.at[h, b, 1], behind)

    def s2(h, b):
        take((h, "Y1", 1, b), y1.at[h, b, 0])
        part[h, rows(b, 1, 0, 32)] += y1[h, b, 0]
        push((h, "Y2", b), part.at[h, rows(b, 1, 0, 64)], y2.at[h, b, 0], ahead)
        take((h, "Y1", -1, b), y1.at[h, b, 1])
        part[h, rows(b, -1, 32, 32)] += y1[h, b, 1]
        push((h, "Y2", b), part.at[h, rows(b, -1, 0, 64)], y2.at[h, b, 1], behind)

    def s3(h, b):
        take((h, "Y2", b), y2.at[h, b])
        ysum[h, b] = part[h, rows(b, 0, 0, 64)] + y2[h, b, 0] + y2[h, b, 1]
        push((h, "X", b), ysum.at[h, b], arx.at[h, b], opposite)

    def s4(h, b):
        take((h, "X", b), arx.at[h, b])
        agg[h, rows(b, 0, 0, 64)] = ysum[h, b] + arx[h, b]
        mine = agg.at[h, rows(b, 0, 0, 64)]
        push((h, "Y3", 1, b), mine, mine, ahead)
        push((h, "Y3", -1, b), mine, mine, behind)

    def s5(h, b):
        take((h, "Y3", 1, b), agg.at[h, pl.ds(0, 64)])
        ref = agg.at[h, rows(b, -1, 0, 32)]
        push((h, "Y4", b), ref, ref, ahead)
        take((h, "Y3", -1, b), agg.at[h, pl.ds(0, 64)])
        ref = agg.at[h, rows(b, 1, 32, 32)]
        push((h, "Y4", b), ref, ref, behind)

    def s6(h, b):
        take((h, "Y4", b), agg.at[h, pl.ds(0, 64)])

    stores = []

    def dense(b):
        span = pl.ds(b * T, T)
        summed = jnp.concatenate([agg[0, span], agg[1, span]], axis=1)
        w = (w_hi[...], w_lo[...])
        pre = dot3(split(summed), w) + bias[...]
        sigma = jax.nn.sigmoid(pre)
        hid[span, :] = pre * sigma
        stores.append(load(hid.at[span], hid_out.at[span]))
        grad = cot_v[span, :] * sigma * (1.0 + pre * (1.0 - sigma))
        gs = split(grad)
        bh, bl = split(dot3(w, gs, 1, 1))
        for t in range(6):
            tile = pl.ds(t * T, T)
            sp = dot3((bh, bl), (a_hi[b, :, tile], a_lo[b, :, tile]))
            spread[b * 6 + t, 0] = sp[:, :128]
            spread[b * 6 + t, 1] = sp[:, 128:]
        gw = dot3(split(summed.T), gs)
        gb = jnp.sum(grad, axis=0, keepdims=True)
        gw_acc[...] = gw if b == 0 else gw_acc[...] + gw
        gb_acc[...] = gb if b == 0 else gb_acc[...] + gb

    ag_init(0)
    prepare_tables()
    ag_step(0, 1)
    ag_init(1)
    prepare(0)
    ag_step(0, 2)
    ag_step(1, 1)
    prepare(1)
    ag_step(0, 3)
    ag_step(1, 2)
    prepare(2)
    ag_step(0, 4)
    ag_step(1, 3)
    prepare(3)
    ag_end(0)
    s1(0, 0)
    s1(0, 1)
    ag_step(1, 4)
    s1(0, 2)
    s1(0, 3)
    s2(0, 0)
    s2(0, 1)
    ag_end(1)
    s2(0, 2)
    s2(0, 3)
    s1(1, 0)
    s3(0, 0)
    s3(0, 1)
    s1(1, 1)
    s3(0, 2)
    s3(0, 3)
    s1(1, 2)
    s2(1, 0)
    s4(0, 0)
    s1(1, 3)
    for b in range(4):
        if b > 0:
            s4(0, b)
            s2(1, b)
    for b in range(4):
        s5(0, b)
        s3(1, b)
    for b in range(4):
        s4(1, b)
    for b in range(4):
        s6(0, b)
        s5(1, b)
    cot_load.wait()
    for b in range(4):
        s6(1, b)
        dense(b)

    gwp[...] = jnp.zeros_like(gwp)
    for c_ in range(2):
        for xl_ in range(2):
            piece = gw_acc[pl.ds(m8(grp * 32 + (xl_ * 2 + c_) * 8), 8), :]
            gwp[c_, xl_, :, pl.ds(0, 256)] = piece * scaling
            gwp[c_, xl_, pl.ds(0, 1), pl.ds(256, 128)] = gb_acc[:, pl.ds(0, 128)] * scaling
            gwp[c_, xl_, pl.ds(1, 1), pl.ds(256, 128)] = gb_acc[:, pl.ds(128, 128)] * scaling
    push("G1", gwp.at[1 - c], g1, twin)

    chip = y * 4 + xh * 2 + xl

    def g_step(i):
        if i == 1:
            take("G1", g1)
            gwp[c] += g1[...]
            push("G2", gwp.at[c, 1 - xl], g2, across)
        elif i == 2:
            take("G2", g2)
            r3[z] = gwp[c, xl] + g2[...]
            for k in range(1, NZ):
                push("G3", r3.at[z], r3.at[z], dev(z_=zz(k)))
        elif i == 3:
            take("G3", r3.at[pl.ds(0, NZ - 1)])
            fin = r3[0]
            for k in range(1, NZ):
                fin = fin + r3[k]
            gb_out[:, pl.ds(0, 128)] = fin[0:1, 256:]
            gb_out[:, pl.ds(128, 128)] = fin[1:2, 256:]
            gwo[chip, c] = fin[:, :256]
            for peer in plane:
                push("G4", gwo.at[chip, c], gwo.at[chip, c], peer)
        elif i == 4:
            take("G4", gwo.at[pl.ds(0, 15), 0])
            push("G5", gwo.at[:, c], gwo.at[:, c], twin)

    def gather(col, half):
        total = None
        for b in range(4):
            at = b * 16 + col
            term = spread[inv[at], half] * msk[at]
            total = term if total is None else total + term
        return total

    slot_of = {o: i for i, o in enumerate((4, 3, -3, 2, -2, 1, -1, 0))}
    lane_of = {1: 0, -1: 1}
    RS_P = T - RS_Q
    p_rows, q_rows = pl.ds(RS_Q, RS_P), pl.ds(0, RS_Q)

    def col_of(o, other):
        return zz(o) * 2 + ((1 - xl) if other else xl)

    def pair_of(o):
        return pl.ds(pl.multiple_of(zz(o) * 2, 2), 2)

    def to_twin(o):
        for other in (True, False):
            col = col_of(o, other)
            g_send[col] = gather(col, 1 - c)
        push(("S", o), g_send.at[pair_of(o)], g_recv.at[pair_of(o)], twin)

    def chip_sum(o):
        take(("S", o), g_recv.at[pair_of(o)])
        for other in (True, False):
            col = col_of(o, other)
            g_own[col] = gather(col, c) + g_recv[col]
            if other:
                push(("RX", o), g_own.at[col, p_rows], rx.at[slot_of[o]], across)

    pieces = {"RQ": (True, 0, 56, lq), "REQ": (False, 0, 56, le), "REP": (False, RS_Q, 72, le)}

    def ring(name, k):
        other, first, count, land = pieces[name]
        turns = [(part, d) for part in range(2) for d in both]
        if k == 4:
            turns = [(part, d) for part, d in turns if part == lane_of[d]]
        if k == 3:
            turns.sort(key=lambda turn: turn[0] == lane_of[turn[1]])
        for part, d in turns:
            span = pl.ds(first + part * count, count)
            col = col_of(d * k, other)
            if k < 3 or (k == 3 and part == lane_of[d]):
                take((name, d, part, k + 1), land.at[lane_of[d], k, span])
                g_own[col, span] += land[lane_of[d], k, span]
            push((name, d, part, k), g_own.at[col, span], land.at[lane_of[d], k - 1, span], along[d])

    def ring_end(name):
        other, first, count, land = pieces[name]
        for part in range(2):
            for d in both:
                take((name, d, part, 1), land.at[lane_of[d], 0, pl.ds(first + part * count, count)])

    def ring_q(k):
        ring("RQ", k)
        ring("REQ", k)

    def ring_p(k):
        for o in (4,) if k == 4 else (k, -k):
            take(("RX", o), rx.at[slot_of[o]])
            g_own[col_of(o, False), p_rows] += rx[slot_of[o]]
        ring("REP", k)

    to_twin(4)
    to_twin(3)
    to_twin(-3)
    chip_sum(4)
    ring_q(4)
    g_step(1)
    to_twin(2)
    to_twin(-2)
    chip_sum(3)
    chip_sum(-3)
    to_twin(1)
    to_twin(-1)
    to_twin(0)
    ring_p(4)
    ring_q(3)
    g_step(2)
    chip_sum(2)
    chip_sum(-2)
    ring_p(3)
    chip_sum(1)
    chip_sum(-1)
    chip_sum(0)
    ring_q(2)
    g_step(3)
    ring_p(2)
    ring_q(1)
    ring_p(1)

    far, near = col_of(0, True), col_of(0, False)
    ring_end("RQ")
    g_own[far, q_rows] += lq[0, 0] + lq[1, 0]
    push("XF", g_own.at[far, q_rows], xq, across)
    g_step(4)
    ring_end("REQ")
    take(("RX", 0), rx.at[slot_of[0]])
    ring_end("REP")
    g_own[near, p_rows] += le[0, 0, p_rows] + le[1, 0, p_rows] + rx[slot_of[0]]
    take("G5", gwo.at[:, 0])
    gw_out[...] = gwo[...].reshape(256, 256)
    take("XF", xq)
    g_own[near, q_rows] += le[0, 0, q_rows] + le[1, 0, q_rows] + xq[...]
    gf_out[...] = g_own[near].T

    assert len(groups) == N_MSG and n_loads[0] == 15
    for store in stores:
        store.wait()
    for copy in sends[-N_SEND:]:
        copy.wait_send()


def deliver(hid, gf, gw, gb, hid_out, gf_out, gw_out, gb_out, hid_v, gf_v, gw_v, gb_v, sem_in, sem_out):
    steps = [(hid.at[pl.ds(i * T, T)], hid_v.at[pl.ds(i * T, T)], hid_out.at[pl.ds(i * T, T)]) for i in range(4)]
    steps += [(gf, gf_v, gf_out), (gw, gw_v, gw_out), (gb, gb_v, gb_out)]
    ins = [pltpu.make_async_copy(a, v, sem_in.at[i]) for i, (a, v, _) in enumerate(steps)]
    outs = [pltpu.make_async_copy(v, o, sem_out.at[i]) for i, (_, v, o) in enumerate(steps)]
    for copy in ins:
        copy.start()
    for first, then in zip(ins, outs):
        first.wait()
        then.start()
    for copy in outs:
        copy.wait()


def on_device(features, tiles, cols, counts, weight, bias, cot):
    n_rows = cot.shape[0]
    scaling = 1.0 / float(n_rows * 32) ** 0.5
    vmem = pl.BlockSpec(memory_space=pltpu.VMEM)
    hbm = pl.BlockSpec(memory_space=pl.ANY)
    shape = jax.ShapeDtypeStruct
    V = pltpu.VMEM
    scratch = [
        V((32, 128, 128), F32), V((32, 128, 128), F32),
        V((4, 6, T, T), F32),
        V((4, T, 6 * T), BF16), V((4, T, 6 * T), BF16),
        V((6 * T, 128), BF16), V((6 * T, 128), BF16),
        V((T, T), F32), V((T, T), BF16), V((T, T), BF16),
        V((1, T), F32),
        V((1024, T), F32),
        V((2, 1024, 128), F32),
        V((2, 4, 2, 32, 128), F32), V((2, 4, 2, 64, 128), F32),
        V((2, 4, 64, 128), F32), V((2, 4, 64, 128), F32),
        V((2, 1024, 128), F32), V((1024, T), F32),
        V((T, T), F32), V((1, T), F32),
        V((24, 2, T, 128), F32),
        V((16, T, 128), F32), V((16, T, 128), F32), V((16, T, 128), F32),
        V((8, T - RS_Q, 128), F32),
        V((2, 4, T, 128), F32), V((2, 4, RS_Q, 128), F32),
        V((RS_Q, 128), F32),
        V((2, 2, 8, 384), F32), V((2, 8, 384), F32), V((8, 384), F32),
        V((8, 8, 384), F32),
        V((16, 2, 8, T), F32),
        pltpu.SMEM((4, 1, 6), jnp.int32), pltpu.SMEM((1, 4), jnp.int32),
        pltpu.SMEM((64,), jnp.int32), pltpu.SMEM((64,), F32),
        pltpu.SemaphoreType.DMA((N_SEND,)), pltpu.SemaphoreType.DMA((N_MSG,)),
        pltpu.SemaphoreType.DMA((15,)),
    ]
    outs = (shape((1024, T), F32), shape((128, T), F32), shape((T, T), F32), shape((1, T), F32))
    results = pl.pallas_call(
        functools.partial(kernel, scaling),
        out_shape=outs,
        in_specs=[hbm] * 7,
        out_specs=(hbm, vmem, vmem, vmem),
        scratch_shapes=scratch,
        compiler_params=pltpu.CompilerParams(
            collective_id=0, has_side_effects=True, vmem_limit_bytes=60 << 20,
        ),
        name="graph_layer",
    )(features, tiles, cols, counts.T, weight, bias.reshape(1, T), cot)
    hid, gf, gw, gb = pl.pallas_call(
        deliver,
        out_shape=outs,
        in_specs=[hbm] * 4,
        out_specs=(hbm,) * 4,
        scratch_shapes=[V(o.shape, F32) for o in outs] + [pltpu.SemaphoreType.DMA((7,))] * 2,
        name="deliver",
    )(*results)
    return hid, gf, gw, gb.reshape(T)


def solution(mesh):
    return jax.shard_map(
        on_device,
        mesh=mesh,
        in_specs=(
            P(("grp", "row"), None),
            P("row", "grp", None, None, None),
            P("row", "grp", None),
            P("row", "grp"),
            P(),
            P(),
            P("row", None),
        ),
        out_specs=(P("row", None), P(("grp", "row"), None), P(), P()),
        check_vma=False,
    )
```

```python
import functools

import jax
import jax.numpy as jnp
from jax import lax
from jax.experimental import pallas as pl
from jax.experimental.pallas import tpu as pltpu
from jax.sharding import PartitionSpec as P

MESH = pl.DeviceIdType.MESH
F32, BF16 = jnp.float32, jnp.bfloat16
NZ, NY = 8, 4
T = 256
AG_Q = 56
RS_Q = 112
N_MSG, N_SEND = 188, 48


def split(x):
    hi = x.astype(BF16)
    return hi, (x - hi.astype(F32)).astype(BF16)


def dot(a, b, ca=1, cb=0):
    return lax.dot_general(a, b, (((ca,), (cb,)), ((), ())), preferred_element_type=F32)


def dot3(a, b, ca=1, cb=0):
    (ah, al), (bh, bl) = a, b
    return dot(ah, bh, ca, cb) + dot(ah, bl, ca, cb) + dot(al, bh, ca, cb)


def kernel(
    scaling,
    feat, tiles, cols_in, counts_in, weight, bias_in, cot,
    hid_out, gf_out, gw_out, gb_out,
    panel_a, panel_b, stage, a_hi, a_lo, x_hi, x_lo, w_v, w_hi, w_lo, bias, cot_v,
    part, y1, y2, ysum, arx, agg, hid, gw_acc, gb_acc,
    spread, g_send, g_own, g_recv, rx, le, lq, xq,
    gwp, g1, g2, r3, gwo, cols, counts, inv, msk,
    send_sem, recv_sem, load_sem,
):
    row, grp = lax.axis_index("row"), lax.axis_index("grp")
    z, xl, c = lax.div(row, 4), lax.rem(lax.div(row, 2), 2), lax.rem(row, 2)
    y, xh = lax.div(grp, 2), lax.rem(grp, 2)

    def zz(k):
        return lax.rem(z + (k + NZ), NZ)

    def yy(k):
        return lax.rem(y + (k + NY), NY)

    def dev(z_=None, xl_=None, c_=None, y_=None, xh_=None):
        z_, xl_, c_ = z if z_ is None else z_, xl if xl_ is None else xl_, c if c_ is None else c_
        y_, xh_ = y if y_ is None else y_, xh if xh_ is None else xh_
        return {"grp": y_ * 2 + xh_, "row": z_ * 4 + xl_ * 2 + c_}

    def blk(z_, xl_, c_):
        return z_ * 4 + xl_ * 2 + c_

    def m8(v):
        return pl.multiple_of(v, 8)

    panels = (panel_a, panel_b)
    sends, groups = [], {}

    def push(group, src, dst, device):
        at, slot = groups.setdefault(group, len(groups)), len(sends) % N_SEND
        if len(sends) >= N_SEND:
            sends[-N_SEND].wait_send()
        copy = pltpu.make_async_remote_copy(
            src_ref=src, dst_ref=dst, send_sem=send_sem.at[slot], recv_sem=recv_sem.at[at],
            device_id=device, device_id_type=MESH,
        )
        copy.start()
        sends.append(copy)

    def take(group, ref):
        pltpu.make_async_copy(ref, ref, recv_sem.at[groups[group]]).wait()

    own = blk(z, xl, c)
    n_loads = [0]

    def load(src, dst):
        copy = pltpu.make_async_copy(src, dst, load_sem.at[n_loads[0]])
        copy.start()
        n_loads[0] += 1
        return copy

    barrier = pltpu.get_barrier_semaphore()
    plane = [
        dev(y_=yy(i // 4), xh_=(1 - xh) if i // 2 % 2 else xh, xl_=(1 - xl) if i % 2 else xl)
        for i in range(1, 16)
    ]
    peers = [dev(z_=zz(1)), dev(z_=zz(-1)), dev(xl_=1 - xl), dev(c_=1 - c)]
    peers += [dev(y_=yy(1)), dev(y_=yy(-1)), dev(xh_=1 - xh)]
    for peer in peers:
        pl.semaphore_signal(barrier, inc=1, device_id=peer, device_id_type=MESH)

    feat_loads = [load(feat.at[:, pl.ds(h * 128, 128)], panels[h].at[own]) for h in range(2)]
    small_loads = [load(cols_in, cols), load(counts_in, counts), load(weight, w_v), load(bias_in, bias)]
    tile_loads = [load(tiles.at[b, 0], stage.at[b]) for b in range(4)]
    cot_load = load(cot, cot_v)
    for copy in feat_loads:
        copy.wait()
    pl.semaphore_wait(barrier, len(peers))

    up, down, across, twin = dev(z_=zz(1)), dev(z_=zz(-1)), dev(xl_=1 - xl), dev(c_=1 - c)
    along = {1: up, -1: down}
    both = (1, -1)
    AG_P = 128 - AG_Q
    ep_half = {1: (AG_Q, 40), -1: (AG_Q + 40, AG_P - 40)}
    eq_half = {1: (0, 32), -1: (32, AG_Q - 32)}

    def same(h, key, at, span, device):
        ref = panels[h].at[at, pl.ds(*span)]
        push((h, *key), ref, ref, device)

    def took(h, key, blocks, count):
        take((h, *key), panels[h].at[pl.ds(0, blocks), pl.ds(0, count)])

    def ag_init(h):
        same(h, ("Q", 0), own, (0, AG_Q), across)
        for d in both:
            same(h, ("EP", d, 1), own, (AG_Q, AG_P), along[d])
        for d in both:
            same(h, ("EQ", d, 1), own, (0, AG_Q), along[d])
        same(h, ("P", 0), own, (AG_Q, AG_P), across)
        same(h, ("SS",), own, (0, 128), twin)

    def ag_crossed(h, o):
        took(h, ("P", o), 1, AG_P)
        same(h, ("SS",), blk(zz(-o), 1 - xl, c), (0, 128), twin)

    def ag_e(h, k):
        for d in both:
            at = blk(zz(-d * k), xl, c)
            took(h, ("EP", d, k), 1, AG_P)
            same(h, ("EP", d, k + 1), at, (AG_Q, AG_P) if k < 3 else ep_half[d], along[d])
            same(h, ("P", d * k), at, (AG_Q, AG_P), across)
        for d in both:
            at = blk(zz(-d * k), xl, c)
            took(h, ("EQ", d, k), 1, AG_Q)
            same(h, ("EQ", d, k + 1), at, (0, AG_Q) if k < 3 else eq_half[d], along[d])
            same(h, ("SS",), at, (0, 128), twin)

    def ag_q(h, k):
        if k == 0:
            took(h, ("Q", 0), 1, AG_Q)
        for d in both:
            at = blk(zz(-d * k), 1 - xl, c)
            if k > 0:
                took(h, ("Q", d, k), 1, AG_Q)
            same(h, ("Q", d, k + 1), at, (0, AG_Q) if k < 3 else eq_half[d], along[d])

    def ag_step(h, k):
        if k < 4:
            ag_e(h, k)
        else:
            at = blk(zz(4), xl, c)
            for d in both:
                took(h, ("EP", d, 4), 1, ep_half[d][1])
            same(h, ("P", 4), at, (AG_Q, AG_P), across)
            for d in both:
                took(h, ("EQ", d, 4), 1, eq_half[d][1])
            same(h, ("SS",), at, (0, 128), twin)
        ag_q(h, k - 1)
        for o in {1: (), 2: (0,), 3: (1, -1), 4: (2, -2)}[k]:
            ag_crossed(h, o)

    def ag_end(h):
        ag_crossed(h, 3)
        ag_crossed(h, -3)
        for d in both:
            took(h, ("Q", d, 4), 1, eq_half[d][1])
        ag_crossed(h, 4)
        took(h, ("SS",), 16, 128)

    def prepare_tables():
        for copy in small_loads:
            copy.wait()
        wh, wl = split(w_v[...])
        w_hi[...] = wh
        w_lo[...] = wl

        @pl.loop(0, 64)
        def _(i):
            b, col = lax.div(i, 16), lax.rem(i, 16)
            slot, live = jnp.int32(0), jnp.float32(0)
            for t in range(6):
                hit = jnp.logical_and(cols[b, 0, t] == col, counts[0, b] > t)
                slot = jnp.where(hit, b * 6 + t, slot)
                live = jnp.where(hit, jnp.float32(1), live)
            inv[i] = slot
            msk[i] = live

    def prepare(b):
        tile_loads[b].wait()
        for t in range(6):
            hi, lo = split(stage[b, t])
            a_hi[b, :, pl.ds(t * T, T)] = hi
            a_lo[b, :, pl.ds(t * T, T)] = lo

    def forward(b):
        for t in range(6):
            at = cols[b, 0, t]
            live = jnp.where(counts[0, b] > t, jnp.float32(1), jnp.float32(0))
            for h in range(2):
                hi, lo = split(panels[h][pl.ds(2 * at, 2)].reshape(T, 128) * live)
                x_hi[pl.ds(t * T, T), pl.ds(h * 128, 128)] = hi
                x_lo[pl.ds(t * T, T), pl.ds(h * 128, 128)] = lo
        total = dot3((a_hi[b], a_lo[b]), (x_hi[...], x_lo[...]))
        for h in range(2):
            part[h, pl.ds(b * T, T), :] = total[:, h * 128 : h * 128 + 128]

    ahead, behind, opposite = dev(y_=yy(1)), dev(y_=yy(-1)), dev(xh_=1 - xh)

    def rows(b, k, first, count):
        return pl.ds(m8(b * T + yy(k) * 64 + first), count)

    def s1(h, b):
        push((h, "Y1", 1, b), part.at[h, rows(b, 2, 0, 32)], y1.at[h, b, 0], ahead)
        push((h, "Y1", -1, b), part.at[h, rows(b, 2, 32, 32)], y1.at[h, b, 1], behind)

    def s2(h, b):
        take((h, "Y1", 1, b), y1.at[h, b, 0])
        part[h, rows(b, 1, 0, 32)] += y1[h, b, 0]
        push((h, "Y2", b), part.at[h, rows(b, 1, 0, 64)], y2.at[h, b, 0], ahead)
        take((h, "Y1", -1, b), y1.at[h, b, 1])
        part[h, rows(b, -1, 32, 32)] += y1[h, b, 1]
        push((h, "Y2", b), part.at[h, rows(b, -1, 0, 64)], y2.at[h, b, 1], behind)

    def s3(h, b):
        take((h, "Y2", b), y2.at[h, b])
        ysum[h, b] = part[h, rows(b, 0, 0, 64)] + y2[h, b, 0] + y2[h, b, 1]
        push((h, "X", b), ysum.at[h, b], arx.at[h, b], opposite)

    def s4(h, b):
        take((h, "X", b), arx.at[h, b])
        agg[h, rows(b, 0, 0, 64)] = ysum[h, b] + arx[h, b]
        mine = agg.at[h, rows(b, 0, 0, 64)]
        push((h, "Y3", 1, b), mine, mine, ahead)
        push((h, "Y3", -1, b), mine, mine, behind)

    def s5(h, b):
        take((h, "Y3", 1, b), agg.at[h, pl.ds(0, 64)])
        ref = agg.at[h, rows(b, -1, 0, 32)]
        push((h, "Y4", b), ref, ref, ahead)
        take((h, "Y3", -1, b), agg.at[h, pl.ds(0, 64)])
        ref = agg.at[h, rows(b, 1, 32, 32)]
        push((h, "Y4", b), ref, ref, behind)

    def s6(h, b):
        take((h, "Y4", b), agg.at[h, pl.ds(0, 64)])

    stores = []

    def dense(b):
        span = pl.ds(b * T, T)
        summed = jnp.concatenate([agg[0, span], agg[1, span]], axis=1)
        w = (w_hi[...], w_lo[...])
        pre = dot3(split(summed), w) + bias[...]
        sigma = jax.nn.sigmoid(pre)
        hid[span, :] = pre * sigma
        stores.append(load(hid.at[span], hid_out.at[span]))
        grad = cot_v[span, :] * sigma * (1.0 + pre * (1.0 - sigma))
        gs = split(grad)
        bh, bl = split(dot3(w, gs, 1, 1))
        for t in range(6):
            tile = pl.ds(t * T, T)
            sp = dot3((bh, bl), (a_hi[b, :, tile], a_lo[b, :, tile]))
            spread[b * 6 + t, 0] = sp[:, :128]
            spread[b * 6 + t, 1] = sp[:, 128:]
        gw = dot3(split(summed.T), gs)
        gb = jnp.sum(grad, axis=0, keepdims=True)
        gw_acc[...] = gw if b == 0 else gw_acc[...] + gw
        gb_acc[...] = gb if b == 0 else gb_acc[...] + gb

    ag_init(0)
    ag_init(1)
    prepare_tables()
    for k in range(1, 5):
        for h in range(2):
            ag_step(h, k)
        prepare(k - 1)
    for h in range(2):
        ag_end(h)
    for b in range(4):
        if b == 3:
            for h in range(2):
                s2(h, 0)
        forward(b)
        for h in range(2):
            s1(h, b)
    for stage in (s2, s3, s4):
        for b in range(1 if stage is s2 else 0, 4):
            for h in range(2):
                stage(h, b)
    for b in range(4):
        if b == 3:
            cot_load.wait()
            for h in range(2):
                s6(h, 0)
            dense(0)
        for h in range(2):
            s5(h, b)
    for b in range(1, 4):
        for h in range(2):
            s6(h, b)
        dense(b)

    gwp[...] = jnp.zeros_like(gwp)
    for c_ in range(2):
        for xl_ in range(2):
            piece = gw_acc[pl.ds(m8(grp * 32 + (xl_ * 2 + c_) * 8), 8), :]
            gwp[c_, xl_, :, pl.ds(0, 256)] = piece * scaling
            gwp[c_, xl_, pl.ds(0, 1), pl.ds(256, 128)] = gb_acc[:, pl.ds(0, 128)] * scaling
            gwp[c_, xl_, pl.ds(1, 1), pl.ds(256, 128)] = gb_acc[:, pl.ds(128, 128)] * scaling
    push("G1", gwp.at[1 - c], g1, twin)

    chip = y * 4 + xh * 2 + xl

    def g_step(i):
        if i == 1:
            take("G1", g1)
            gwp[c] += g1[...]
            push("G2", gwp.at[c, 1 - xl], g2, across)
        elif i == 2:
            take("G2", g2)
            r3[z] = gwp[c, xl] + g2[...]
            for k in range(1, NZ):
                push("G3", r3.at[z], r3.at[z], dev(z_=zz(k)))
        elif i == 3:
            take("G3", r3.at[pl.ds(0, NZ - 1)])
            fin = r3[0]
            for k in range(1, NZ):
                fin = fin + r3[k]
            gb_out[:, pl.ds(0, 128)] = fin[0:1, 256:]
            gb_out[:, pl.ds(128, 128)] = fin[1:2, 256:]
            gwo[chip, c] = fin[:, :256]
            for peer in plane:
                push("G4", gwo.at[chip, c], gwo.at[chip, c], peer)
        elif i == 4:
            take("G4", gwo.at[pl.ds(0, 15), 0])
            push("G5", gwo.at[:, c], gwo.at[:, c], twin)

    def gather(col, half):
        total = None
        for b in range(4):
            at = b * 16 + col
            term = spread[inv[at], half] * msk[at]
            total = term if total is None else total + term
        return total

    slot_of = {o: i for i, o in enumerate((4, 3, -3, 2, -2, 1, -1, 0))}
    lane_of = {1: 0, -1: 1}
    RS_P = T - RS_Q
    p_rows, q_rows = pl.ds(RS_Q, RS_P), pl.ds(0, RS_Q)

    def col_of(o, other):
        return zz(o) * 2 + ((1 - xl) if other else xl)

    def pair_of(o):
        return pl.ds(pl.multiple_of(zz(o) * 2, 2), 2)

    def to_twin(o):
        for other in (True, False):
            col = col_of(o, other)
            g_send[col] = gather(col, 1 - c)
        push(("S", o), g_send.at[pair_of(o)], g_recv.at[pair_of(o)], twin)

    def chip_sum(o):
        take(("S", o), g_recv.at[pair_of(o)])
        for other in (True, False):
            col = col_of(o, other)
            g_own[col] = gather(col, c) + g_recv[col]
            if other:
                push(("RX", o), g_own.at[col, p_rows], rx.at[slot_of[o]], across)

    pieces = {"RQ": (True, 0, 56, lq), "REQ": (False, 0, 56, le), "REP": (False, RS_Q, 72, le)}

    def ring(name, k):
        other, first, count, land = pieces[name]
        turns = [(part, d) for part in range(2) for d in both]
        if k == 4:
            turns = [(part, d) for part, d in turns if part == lane_of[d]]
        if k == 3:
            turns.sort(key=lambda turn: turn[0] == lane_of[turn[1]])
        for part, d in turns:
            span = pl.ds(first + part * count, count)
            col = col_of(d * k, other)
            if k < 3 or (k == 3 and part == lane_of[d]):
                take((name, d, part, k + 1), land.at[lane_of[d], k, span])
                g_own[col, span] += land[lane_of[d], k, span]
            push((name, d, part, k), g_own.at[col, span], land.at[lane_of[d], k - 1, span], along[d])

    def ring_end(name):
        other, first, count, land = pieces[name]
        for part in range(2):
            for d in both:
                take((name, d, part, 1), land.at[lane_of[d], 0, pl.ds(first + part * count, count)])

    def ring_q(k):
        ring("RQ", k)
        ring("REQ", k)

    def ring_p(k):
        for o in (4,) if k == 4 else (k, -k):
            take(("RX", o), rx.at[slot_of[o]])
            g_own[col_of(o, False), p_rows] += rx[slot_of[o]]
        ring("REP", k)

    to_twin(4)
    to_twin(3)
    to_twin(-3)
    chip_sum(4)
    ring_q(4)
    g_step(1)
    to_twin(2)
    to_twin(-2)
    chip_sum(3)
    chip_sum(-3)
    to_twin(1)
    to_twin(-1)
    to_twin(0)
    ring_p(4)
    ring_q(3)
    g_step(2)
    chip_sum(2)
    chip_sum(-2)
    ring_p(3)
    chip_sum(1)
    chip_sum(-1)
    chip_sum(0)
    ring_q(2)
    g_step(3)
    ring_p(2)
    ring_q(1)
    ring_p(1)

    far, near = col_of(0, True), col_of(0, False)
    ring_end("RQ")
    g_own[far, q_rows] += lq[0, 0] + lq[1, 0]
    push("XF", g_own.at[far, q_rows], xq, across)
    g_step(4)
    ring_end("REQ")
    take(("RX", 0), rx.at[slot_of[0]])
    ring_end("REP")
    g_own[near, p_rows] += le[0, 0, p_rows] + le[1, 0, p_rows] + rx[slot_of[0]]
    take("G5", gwo.at[:, 0])
    gw_out[...] = gwo[...].reshape(256, 256)
    take("XF", xq)
    g_own[near, q_rows] += le[0, 0, q_rows] + le[1, 0, q_rows] + xq[...]
    gf_out[...] = g_own[near].T

    assert len(groups) == N_MSG and n_loads[0] == 15
    for store in stores:
        store.wait()
    for copy in sends[-N_SEND:]:
        copy.wait_send()


def deliver(hid, gf, gw, gb, hid_out, gf_out, gw_out, gb_out, hid_v, gf_v, gw_v, gb_v, sem_in, sem_out):
    steps = [(hid.at[pl.ds(i * T, T)], hid_v.at[pl.ds(i * T, T)], hid_out.at[pl.ds(i * T, T)]) for i in range(4)]
    steps += [(gf, gf_v, gf_out), (gw, gw_v, gw_out), (gb, gb_v, gb_out)]
    ins = [pltpu.make_async_copy(a, v, sem_in.at[i]) for i, (a, v, _) in enumerate(steps)]
    outs = [pltpu.make_async_copy(v, o, sem_out.at[i]) for i, (_, v, o) in enumerate(steps)]
    for copy in ins:
        copy.start()
    for first, then in zip(ins, outs):
        first.wait()
        then.start()
    for copy in outs:
        copy.wait()


def on_device(features, tiles, cols, counts, weight, bias, cot):
    n_rows = cot.shape[0]
    scaling = 1.0 / float(n_rows * 32) ** 0.5
    vmem = pl.BlockSpec(memory_space=pltpu.VMEM)
    hbm = pl.BlockSpec(memory_space=pl.ANY)
    shape = jax.ShapeDtypeStruct
    V = pltpu.VMEM
    scratch = [
        V((32, 128, 128), F32), V((32, 128, 128), F32),
        V((4, 6, T, T), F32),
        V((4, T, 6 * T), BF16), V((4, T, 6 * T), BF16),
        V((6 * T, T), BF16), V((6 * T, T), BF16),
        V((T, T), F32), V((T, T), BF16), V((T, T), BF16),
        V((1, T), F32),
        V((1024, T), F32),
        V((2, 1024, 128), F32),
        V((2, 4, 2, 32, 128), F32), V((2, 4, 2, 64, 128), F32),
        V((2, 4, 64, 128), F32), V((2, 4, 64, 128), F32),
        V((2, 1024, 128), F32), V((1024, T), F32),
        V((T, T), F32), V((1, T), F32),
        V((24, 2, T, 128), F32),
        V((16, T, 128), F32), V((16, T, 128), F32), V((16, T, 128), F32),
        V((8, T - RS_Q, 128), F32),
        V((2, 4, T, 128), F32), V((2, 4, RS_Q, 128), F32),
        V((RS_Q, 128), F32),
        V((2, 2, 8, 384), F32), V((2, 8, 384), F32), V((8, 384), F32),
        V((8, 8, 384), F32),
        V((16, 2, 8, T), F32),
        pltpu.SMEM((4, 1, 6), jnp.int32), pltpu.SMEM((1, 4), jnp.int32),
        pltpu.SMEM((64,), jnp.int32), pltpu.SMEM((64,), F32),
        pltpu.SemaphoreType.DMA((N_SEND,)), pltpu.SemaphoreType.DMA((N_MSG,)),
        pltpu.SemaphoreType.DMA((15,)),
    ]
    outs = (shape((1024, T), F32), shape((128, T), F32), shape((T, T), F32), shape((1, T), F32))
    results = pl.pallas_call(
        functools.partial(kernel, scaling),
        out_shape=outs,
        in_specs=[hbm] * 7,
        out_specs=(hbm, vmem, vmem, vmem),
        scratch_shapes=scratch,
        compiler_params=pltpu.CompilerParams(
            collective_id=0, has_side_effects=True, vmem_limit_bytes=60 << 20,
        ),
        name="graph_layer",
    )(features, tiles, cols, counts.T, weight, bias.reshape(1, T), cot)
    hid, gf, gw, gb = pl.pallas_call(
        deliver,
        out_shape=outs,
        in_specs=[hbm] * 4,
        out_specs=(hbm,) * 4,
        scratch_shapes=[V(o.shape, F32) for o in outs] + [pltpu.SemaphoreType.DMA((7,))] * 2,
        name="deliver",
    )(*results)
    return hid, gf, gw, gb.reshape(T)


def solution(mesh):
    return jax.shard_map(
        on_device,
        mesh=mesh,
        in_specs=(
            P(("grp", "row"), None),
            P("row", "grp", None, None, None),
            P("row", "grp", None),
            P("row", "grp"),
            P(),
            P(),
            P("row", None),
        ),
        out_specs=(P("row", None), P(("grp", "row"), None), P(), P()),
        check_vma=False,
    )
```

```python
import functools

import jax
import jax.numpy as jnp
from jax import lax
from jax.experimental import pallas as pl
from jax.experimental.pallas import tpu as pltpu
from jax.sharding import PartitionSpec as P

MESH = pl.DeviceIdType.MESH
F32, BF16 = jnp.float32, jnp.bfloat16
NZ, NY = 8, 4
T = 256
AG_Q = 56
RS_Q = 112
N_MSG, N_SEND = 189, 36


def split(x):
    hi = x.astype(BF16)
    return hi, (x - hi.astype(F32)).astype(BF16)


def dot(a, b, ca=1, cb=0):
    return lax.dot_general(a, b, (((ca,), (cb,)), ((), ())), preferred_element_type=F32)


def dot3(a, b, ca=1, cb=0):
    (ah, al), (bh, bl) = a, b
    return dot(ah, bh, ca, cb) + dot(ah, bl, ca, cb) + dot(al, bh, ca, cb)


def kernel(
    scaling,
    feat, tiles, cols_in, counts_in, weight, bias_in, cot,
    hid_out, gf_out, gw_out, gb_out,
    panel_a, panel_b, stage, a_hi, a_lo, x_hi, x_lo, w_v, w_hi, w_lo, bias, cot_v,
    part, y1, y2, ysum, arx, agg, hid, gw_acc, gb_acc,
    spread, g_send, g_own, g_recv, rx, le, lq, xq,
    gwp, g1, g2, r3, gwo, cols, counts, inv, msk,
    send_sem, recv_sem, load_sem,
):
    row, grp = lax.axis_index("row"), lax.axis_index("grp")
    z, xl, c = lax.div(row, 4), lax.rem(lax.div(row, 2), 2), lax.rem(row, 2)
    y, xh = lax.div(grp, 2), lax.rem(grp, 2)

    def zz(k):
        return lax.rem(z + (k + NZ), NZ)

    def yy(k):
        return lax.rem(y + (k + NY), NY)

    def dev(z_=None, xl_=None, c_=None, y_=None, xh_=None):
        z_, xl_, c_ = z if z_ is None else z_, xl if xl_ is None else xl_, c if c_ is None else c_
        y_, xh_ = y if y_ is None else y_, xh if xh_ is None else xh_
        return {"grp": y_ * 2 + xh_, "row": z_ * 4 + xl_ * 2 + c_}

    def blk(z_, xl_, c_):
        return z_ * 4 + xl_ * 2 + c_

    def m8(v):
        return pl.multiple_of(v, 8)

    panels = (panel_a, panel_b)
    sends, groups = [], {}

    def push(group, src, dst, device):
        at, slot = groups.setdefault(group, len(groups)), len(sends) % N_SEND
        if len(sends) >= N_SEND:
            sends[-N_SEND].wait_send()
        copy = pltpu.make_async_remote_copy(
            src_ref=src, dst_ref=dst, send_sem=send_sem.at[slot], recv_sem=recv_sem.at[at],
            device_id=device, device_id_type=MESH,
        )
        copy.start()
        sends.append(copy)

    def take(group, ref):
        pltpu.make_async_copy(ref, ref, recv_sem.at[groups[group]]).wait()

    own = blk(z, xl, c)
    n_loads = [0]

    def load(src, dst):
        copy = pltpu.make_async_copy(src, dst, load_sem.at[n_loads[0]])
        copy.start()
        n_loads[0] += 1
        return copy

    barrier = pltpu.get_barrier_semaphore()
    plane = [
        dev(y_=yy(i // 4), xh_=(1 - xh) if i // 2 % 2 else xh, xl_=(1 - xl) if i % 2 else xl)
        for i in range(1, 16)
    ]
    peers = [dev(z_=zz(1)), dev(z_=zz(-1)), dev(xl_=1 - xl), dev(c_=1 - c)]
    peers += [dev(y_=yy(1)), dev(y_=yy(-1)), dev(xh_=1 - xh)]
    for peer in peers:
        pl.semaphore_signal(barrier, inc=1, device_id=peer, device_id_type=MESH)

    feat_loads = [load(feat.at[:, pl.ds(h * 128, 128)], panels[h].at[own]) for h in range(2)]
    small_loads = [load(cols_in, cols), load(counts_in, counts), load(weight, w_v), load(bias_in, bias)]
    tile_loads = [load(tiles.at[b, 0], stage.at[b]) for b in range(4)]
    cot_load = load(cot, cot_v)
    for copy in feat_loads:
        copy.wait()
    pl.semaphore_wait(barrier, len(peers))

    up, down, across, twin = dev(z_=zz(1)), dev(z_=zz(-1)), dev(xl_=1 - xl), dev(c_=1 - c)
    along = {1: up, -1: down}
    both = (1, -1)
    AG_P = 128 - AG_Q
    ep_half = {1: (AG_Q, 40), -1: (AG_Q + 40, AG_P - 40)}
    eq_half = {1: (0, 32), -1: (32, AG_Q - 32)}

    def same(h, key, at, span, device):
        ref = panels[h].at[at, pl.ds(*span)]
        push((h, *key), ref, ref, device)

    def took(h, key, blocks, count):
        take((h, *key), panels[h].at[pl.ds(0, blocks), pl.ds(0, count)])

    def ag_init(h):
        same(h, ("Q", 0), own, (0, AG_Q), across)
        for d in both:
            same(h, ("EP", d, 1), own, (AG_Q, AG_P), along[d])
        for d in both:
            same(h, ("EQ", d, 1), own, (0, AG_Q), along[d])
        same(h, ("P", 0), own, (AG_Q, AG_P), across)
        same(h, ("SS",), own, (0, 128), twin)

    def ag_crossed(h, o):
        took(h, ("P", o), 1, AG_P)
        same(h, ("SS",), blk(zz(-o), 1 - xl, c), (0, 128), twin)

    def ag_e(h, k):
        for d in both:
            at = blk(zz(-d * k), xl, c)
            took(h, ("EP", d, k), 1, AG_P)
            same(h, ("EP", d, k + 1), at, (AG_Q, AG_P) if k < 3 else ep_half[d], along[d])
            same(h, ("P", d * k), at, (AG_Q, AG_P), across)
        for d in both:
            at = blk(zz(-d * k), xl, c)
            took(h, ("EQ", d, k), 1, AG_Q)
            same(h, ("EQ", d, k + 1), at, (0, AG_Q) if k < 3 else eq_half[d], along[d])
            same(h, ("SS",), at, (0, 128), twin)

    def ag_q(h, k):
        if k == 0:
            took(h, ("Q", 0), 1, AG_Q)
        for d in both:
            at = blk(zz(-d * k), 1 - xl, c)
            if k > 0:
                took(h, ("Q", d, k), 1, AG_Q)
            same(h, ("Q", d, k + 1), at, (0, AG_Q) if k < 3 else eq_half[d], along[d])

    def ag_step(h, k):
        if k < 4:
            ag_e(h, k)
        else:
            at = blk(zz(4), xl, c)
            for d in both:
                took(h, ("EP", d, 4), 1, ep_half[d][1])
            same(h, ("P", 4), at, (AG_Q, AG_P), across)
            for d in both:
                took(h, ("EQ", d, 4), 1, eq_half[d][1])
            same(h, ("SS",), at, (0, 128), twin)
        ag_q(h, k - 1)
        for o in {1: (), 2: (0,), 3: (1, -1), 4: (2, -2)}[k]:
            ag_crossed(h, o)

    def ag_end(h):
        ag_crossed(h, 3)
        ag_crossed(h, -3)
        for d in both:
            took(h, ("Q", d, 4), 1, eq_half[d][1])
        ag_crossed(h, 4)
        took(h, ("SS",), 16, 128)

    def prepare_tables():
        for copy in small_loads:
            copy.wait()
        wh, wl = split(w_v[...])
        w_hi[...] = wh
        w_lo[...] = wl

        @pl.loop(0, 64)
        def _(i):
            b, col = lax.div(i, 16), lax.rem(i, 16)
            slot, live = jnp.int32(0), jnp.float32(0)
            for t in range(6):
                hit = jnp.logical_and(cols[b, 0, t] == col, counts[0, b] > t)
                slot = jnp.where(hit, b * 6 + t, slot)
                live = jnp.where(hit, jnp.float32(1), live)
            inv[i] = slot
            msk[i] = live

    def prepare(b):
        tile_loads[b].wait()
        for t in range(6):
            hi, lo = split(stage[b, t])
            a_hi[b, :, pl.ds(t * T, T)] = hi
            a_lo[b, :, pl.ds(t * T, T)] = lo

    def forward(b):
        for t in range(6):
            at = cols[b, 0, t]
            live = jnp.where(counts[0, b] > t, jnp.float32(1), jnp.float32(0))
            for h in range(2):
                hi, lo = split(panels[h][pl.ds(2 * at, 2)].reshape(T, 128) * live)
                x_hi[pl.ds(t * T, T), pl.ds(h * 128, 128)] = hi
                x_lo[pl.ds(t * T, T), pl.ds(h * 128, 128)] = lo
        total = dot3((a_hi[b], a_lo[b]), (x_hi[...], x_lo[...]))
        for h in range(2):
            part[h, pl.ds(b * T, T), :] = total[:, h * 128 : h * 128 + 128]

    ahead, behind, opposite = dev(y_=yy(1)), dev(y_=yy(-1)), dev(xh_=1 - xh)

    def rows(b, k, first, count):
        return pl.ds(m8(b * T + yy(k) * 64 + first), count)

    def s1(h, b):
        push((h, "Y1", 1, b), part.at[h, rows(b, 2, 0, 32)], y1.at[h, b, 0], ahead)
        push((h, "Y1", -1, b), part.at[h, rows(b, 2, 32, 32)], y1.at[h, b, 1], behind)

    def s2(h, b):
        take((h, "Y1", 1, b), y1.at[h, b, 0])
        part[h, rows(b, 1, 0, 32)] += y1[h, b, 0]
        push((h, "Y2", b), part.at[h, rows(b, 1, 0, 64)], y2.at[h, b, 0], ahead)
        take((h, "Y1", -1, b), y1.at[h, b, 1])
        part[h, rows(b, -1, 32, 32)] += y1[h, b, 1]
        push((h, "Y2", b), part.at[h, rows(b, -1, 0, 64)], y2.at[h, b, 1], behind)

    def s3(h, b):
        take((h, "Y2", b), y2.at[h, b])
        ysum[h, b] = part[h, rows(b, 0, 0, 64)] + y2[h, b, 0] + y2[h, b, 1]
        push((h, "X", b), ysum.at[h, b], arx.at[h, b], opposite)

    def s4(h, b):
        take((h, "X", b), arx.at[h, b])
        agg[h, rows(b, 0, 0, 64)] = ysum[h, b] + arx[h, b]
        mine = agg.at[h, rows(b, 0, 0, 64)]
        push((h, "Y3", 1, b), mine, mine, ahead)
        push((h, "Y3", -1, b), mine, mine, behind)

    def s5(h, b):
        take((h, "Y3", 1, b), agg.at[h, pl.ds(0, 64)])
        ref = agg.at[h, rows(b, -1, 0, 32)]
        push((h, "Y4", b), ref, ref, ahead)
        take((h, "Y3", -1, b), agg.at[h, pl.ds(0, 64)])
        ref = agg.at[h, rows(b, 1, 32, 32)]
        push((h, "Y4", b), ref, ref, behind)

    def s6(h, b):
        take((h, "Y4", b), agg.at[h, pl.ds(0, 64)])

    stores = []

    def dense(b):
        span = pl.ds(b * T, T)
        summed = jnp.concatenate([agg[0, span], agg[1, span]], axis=1)
        w = (w_hi[...], w_lo[...])
        pre = dot3(split(summed), w) + bias[...]
        sigma = jax.nn.sigmoid(pre)
        hid[span, :] = pre * sigma
        stores.append(load(hid.at[span], hid_out.at[span]))
        grad = cot_v[span, :] * sigma * (1.0 + pre * (1.0 - sigma))
        gs = split(grad)
        bh, bl = split(dot3(w, gs, 1, 1))
        for t in range(6):
            tile = pl.ds(t * T, T)
            sp = dot3((bh, bl), (a_hi[b, :, tile], a_lo[b, :, tile]))
            spread[b * 6 + t, 0] = sp[:, :128]
            spread[b * 6 + t, 1] = sp[:, 128:]
        gw = dot3(split(summed.T), gs)
        gb = jnp.sum(grad, axis=0, keepdims=True)
        gw_acc[...] = gw if b == 0 else gw_acc[...] + gw
        gb_acc[...] = gb if b == 0 else gb_acc[...] + gb

    ag_init(0)
    ag_init(1)
    prepare_tables()
    for k in range(1, 5):
        for h in range(2):
            ag_step(h, k)
        prepare(k - 1)
    for h in range(2):
        ag_end(h)
    for b in range(4):
        forward(b)
        for h in range(2):
            s1(h, b)
    for stage in (s2, s3, s4, s5):
        for b in range(4):
            for h in range(2):
                stage(h, b)
    cot_load.wait()
    for b in range(4):
        for h in range(2):
            s6(h, b)
        dense(b)

    gwp[...] = jnp.zeros_like(gwp)
    for c_ in range(2):
        for xl_ in range(2):
            piece = gw_acc[pl.ds(m8(grp * 32 + (xl_ * 2 + c_) * 8), 8), :]
            gwp[c_, xl_, :, pl.ds(0, 256)] = piece * scaling
            gwp[c_, xl_, pl.ds(0, 1), pl.ds(256, 128)] = gb_acc[:, pl.ds(0, 128)] * scaling
            gwp[c_, xl_, pl.ds(1, 1), pl.ds(256, 128)] = gb_acc[:, pl.ds(128, 128)] * scaling
    push("G1", gwp.at[1 - c], g1, twin)

    chip = y * 4 + xh * 2 + xl

    def g_step(i):
        if i == 1:
            take("G1", g1)
            gwp[c] += g1[...]
            push("G2", gwp.at[c, 1 - xl], g2, across)
        elif i == 2:
            take("G2", g2)
            r3[z] = gwp[c, xl] + g2[...]
            for k in range(1, NZ):
                push("G3", r3.at[z], r3.at[z], dev(z_=zz(k)))
        elif i == 3:
            take("G3", r3.at[pl.ds(0, NZ - 1)])
            fin = r3[0]
            for k in range(1, NZ):
                fin = fin + r3[k]
            gb_out[:, pl.ds(0, 128)] = fin[0:1, 256:]
            gb_out[:, pl.ds(128, 128)] = fin[1:2, 256:]
            gwo[chip, c] = fin[:, :256]
            for peer in plane:
                push("G4", gwo.at[chip, c], gwo.at[chip, c], peer)
        elif i == 4:
            take("G4", gwo.at[pl.ds(0, 15), 0])
            push("G5", gwo.at[:, c], gwo.at[:, c], twin)

    def gather(col, half):
        total = None
        for b in range(4):
            at = b * 16 + col
            term = spread[inv[at], half] * msk[at]
            total = term if total is None else total + term
        return total

    slot_of = {o: i for i, o in enumerate((4, 3, -3, 2, -2, 1, -1, 0))}
    lane_of = {1: 0, -1: 1}
    RS_P = T - RS_Q
    p_rows, q_rows = pl.ds(RS_Q, RS_P), pl.ds(0, RS_Q)

    def col_of(o, other):
        return zz(o) * 2 + ((1 - xl) if other else xl)

    def pair_of(o):
        return pl.ds(pl.multiple_of(zz(o) * 2, 2), 2)

    def to_twin(o):
        for other in (True, False):
            col = col_of(o, other)
            g_send[col] = gather(col, 1 - c)
        push(("S", o), g_send.at[pair_of(o)], g_recv.at[pair_of(o)], twin)

    def chip_sum(o):
        take(("S", o), g_recv.at[pair_of(o)])
        for other in (True, False):
            col = col_of(o, other)
            g_own[col] = gather(col, c) + g_recv[col]
            if other:
                push(("RX", o), g_own.at[col, p_rows], rx.at[slot_of[o]], across)

    pieces = {"RQ": (True, 0, 56, lq), "REQ": (False, 0, 56, le), "REP": (False, RS_Q, 72, le)}

    def ring(name, k):
        other, first, count, land = pieces[name]
        turns = [(part, d) for part in range(2) for d in both]
        if k == 4:
            turns = [(part, d) for part, d in turns if part == lane_of[d]]
        if k == 3:
            turns.sort(key=lambda turn: turn[0] == lane_of[turn[1]])
        for part, d in turns:
            span = pl.ds(first + part * count, count)
            col = col_of(d * k, other)
            if k < 3 or (k == 3 and part == lane_of[d]):
                take((name, d, part, k + 1), land.at[lane_of[d], k, span])
                g_own[col, span] += land[lane_of[d], k, span]
            push((name, d, part, k), g_own.at[col, span], land.at[lane_of[d], k - 1, span], along[d])

    def ring_end(name, part):
        other, first, count, land = pieces[name]
        for d in both:
            take((name, d, part, 1), land.at[lane_of[d], 0, pl.ds(first + part * count, count)])

    def ring_q(k):
        ring("RQ", k)
        ring("REQ", k)

    def ring_p(k):
        for o in (4,) if k == 4 else (k, -k):
            take(("RX", o), rx.at[slot_of[o]])
            g_own[col_of(o, False), p_rows] += rx[slot_of[o]]
        ring("REP", k)

    to_twin(4)
    to_twin(3)
    to_twin(-3)
    chip_sum(4)
    ring_q(4)
    g_step(1)
    to_twin(2)
    to_twin(-2)
    chip_sum(3)
    chip_sum(-3)
    to_twin(1)
    to_twin(-1)
    to_twin(0)
    ring_p(4)
    ring_q(3)
    g_step(2)
    chip_sum(2)
    chip_sum(-2)
    ring_p(3)
    chip_sum(1)
    chip_sum(-1)
    chip_sum(0)
    ring_q(2)
    g_step(3)
    ring_p(2)
    ring_q(1)
    ring_p(1)

    far, near = col_of(0, True), col_of(0, False)
    for part in range(2):
        ring_end("RQ", part)
        span = pl.ds(part * 56, 56)
        g_own[far, span] += lq[0, 0, span] + lq[1, 0, span]
        push(("XF", part), g_own.at[far, span], xq.at[span], across)
    g_step(4)
    for part in range(2):
        ring_end("REQ", part)
    take(("RX", 0), rx.at[slot_of[0]])
    for part in range(2):
        ring_end("REP", part)
    g_own[near, p_rows] += le[0, 0, p_rows] + le[1, 0, p_rows] + rx[slot_of[0]]
    take("G5", gwo.at[:, 0])
    gw_out[...] = gwo[...].reshape(256, 256)
    for part in range(2):
        take(("XF", part), xq.at[pl.ds(part * 56, 56)])
    g_own[near, q_rows] += le[0, 0, q_rows] + le[1, 0, q_rows] + xq[...]
    gf_out[...] = g_own[near].T

    assert len(groups) == N_MSG and n_loads[0] == 15
    for store in stores:
        store.wait()
    for copy in sends[-N_SEND:]:
        copy.wait_send()


def deliver(hid, gf, gw, gb, hid_out, gf_out, gw_out, gb_out, hid_v, gf_v, gw_v, gb_v, sem_in, sem_out):
    steps = [(hid.at[pl.ds(i * T, T)], hid_v.at[pl.ds(i * T, T)], hid_out.at[pl.ds(i * T, T)]) for i in range(4)]
    steps += [(gf, gf_v, gf_out), (gw, gw_v, gw_out), (gb, gb_v, gb_out)]
    ins = [pltpu.make_async_copy(a, v, sem_in.at[i]) for i, (a, v, _) in enumerate(steps)]
    outs = [pltpu.make_async_copy(v, o, sem_out.at[i]) for i, (_, v, o) in enumerate(steps)]
    for copy in ins:
        copy.start()
    for first, then in zip(ins, outs):
        first.wait()
        then.start()
    for copy in outs:
        copy.wait()


def on_device(features, tiles, cols, counts, weight, bias, cot):
    n_rows = cot.shape[0]
    scaling = 1.0 / float(n_rows * 32) ** 0.5
    vmem = pl.BlockSpec(memory_space=pltpu.VMEM)
    hbm = pl.BlockSpec(memory_space=pl.ANY)
    shape = jax.ShapeDtypeStruct
    V = pltpu.VMEM
    scratch = [
        V((32, 128, 128), F32), V((32, 128, 128), F32),
        V((4, 6, T, T), F32),
        V((4, T, 6 * T), BF16), V((4, T, 6 * T), BF16),
        V((6 * T, T), BF16), V((6 * T, T), BF16),
        V((T, T), F32), V((T, T), BF16), V((T, T), BF16),
        V((1, T), F32),
        V((1024, T), F32),
        V((2, 1024, 128), F32),
        V((2, 4, 2, 32, 128), F32), V((2, 4, 2, 64, 128), F32),
        V((2, 4, 64, 128), F32), V((2, 4, 64, 128), F32),
        V((2, 1024, 128), F32), V((1024, T), F32),
        V((T, T), F32), V((1, T), F32),
        V((24, 2, T, 128), F32),
        V((16, T, 128), F32), V((16, T, 128), F32), V((16, T, 128), F32),
        V((8, T - RS_Q, 128), F32),
        V((2, 4, T, 128), F32), V((2, 4, RS_Q, 128), F32),
        V((RS_Q, 128), F32),
        V((2, 2, 8, 384), F32), V((2, 8, 384), F32), V((8, 384), F32),
        V((8, 8, 384), F32),
        V((16, 2, 8, T), F32),
        pltpu.SMEM((4, 1, 6), jnp.int32), pltpu.SMEM((1, 4), jnp.int32),
        pltpu.SMEM((64,), jnp.int32), pltpu.SMEM((64,), F32),
        pltpu.SemaphoreType.DMA((N_SEND,)), pltpu.SemaphoreType.DMA((N_MSG,)),
        pltpu.SemaphoreType.DMA((15,)),
    ]
    outs = (shape((1024, T), F32), shape((128, T), F32), shape((T, T), F32), shape((1, T), F32))
    results = pl.pallas_call(
        functools.partial(kernel, scaling),
        out_shape=outs,
        in_specs=[hbm] * 7,
        out_specs=(hbm, vmem, vmem, vmem),
        scratch_shapes=scratch,
        compiler_params=pltpu.CompilerParams(
            collective_id=0, has_side_effects=True, vmem_limit_bytes=60 << 20,
        ),
        name="graph_layer",
    )(features, tiles, cols, counts.T, weight, bias.reshape(1, T), cot)
    hid, gf, gw, gb = pl.pallas_call(
        deliver,
        out_shape=outs,
        in_specs=[hbm] * 4,
        out_specs=(hbm,) * 4,
        scratch_shapes=[V(o.shape, F32) for o in outs] + [pltpu.SemaphoreType.DMA((7,))] * 2,
        name="deliver",
    )(*results)
    return hid, gf, gw, gb.reshape(T)


def solution(mesh):
    return jax.shard_map(
        on_device,
        mesh=mesh,
        in_specs=(
            P(("grp", "row"), None),
            P("row", "grp", None, None, None),
            P("row", "grp", None),
            P("row", "grp"),
            P(),
            P(),
            P("row", None),
        ),
        out_specs=(P("row", None), P(("grp", "row"), None), P(), P()),
        check_vma=False,
    )
```

```python
import functools

import jax
import jax.numpy as jnp
from jax import lax
from jax.experimental import pallas as pl
from jax.experimental.pallas import tpu as pltpu
from jax.sharding import PartitionSpec as P

MESH = pl.DeviceIdType.MESH
F32, BF16 = jnp.float32, jnp.bfloat16
NZ, NY = 8, 4
T = 256
AG_Q = 48
RS_Q = 112
N_MSG, N_SEND = 189, 36


def split(x):
    hi = x.astype(BF16)
    return hi, (x - hi.astype(F32)).astype(BF16)


def dot(a, b, ca=1, cb=0):
    return lax.dot_general(a, b, (((ca,), (cb,)), ((), ())), preferred_element_type=F32)


def dot3(a, b, ca=1, cb=0):
    (ah, al), (bh, bl) = a, b
    return dot(ah, bh, ca, cb) + dot(ah, bl, ca, cb) + dot(al, bh, ca, cb)


def kernel(
    scaling,
    feat, tiles, cols_in, counts_in, weight, bias_in, cot,
    hid_out, gf_out, gw_out, gb_out,
    panel_a, panel_b, stage, a_hi, a_lo, x_hi, x_lo, w_v, w_hi, w_lo, bias, cot_v,
    part, y1, y2, ysum, arx, agg, hid, gw_acc, gb_acc,
    spread, g_send, g_own, g_recv, rx, le, lq, xq,
    gwp, g1, g2, r3, gwo, cols, counts, inv, msk,
    send_sem, recv_sem, load_sem,
):
    row, grp = lax.axis_index("row"), lax.axis_index("grp")
    z, xl, c = lax.div(row, 4), lax.rem(lax.div(row, 2), 2), lax.rem(row, 2)
    y, xh = lax.div(grp, 2), lax.rem(grp, 2)

    def zz(k):
        return lax.rem(z + (k + NZ), NZ)

    def yy(k):
        return lax.rem(y + (k + NY), NY)

    def dev(z_=None, xl_=None, c_=None, y_=None, xh_=None):
        z_, xl_, c_ = z if z_ is None else z_, xl if xl_ is None else xl_, c if c_ is None else c_
        y_, xh_ = y if y_ is None else y_, xh if xh_ is None else xh_
        return {"grp": y_ * 2 + xh_, "row": z_ * 4 + xl_ * 2 + c_}

    def blk(z_, xl_, c_):
        return z_ * 4 + xl_ * 2 + c_

    def m8(v):
        return pl.multiple_of(v, 8)

    panels = (panel_a, panel_b)
    sends, groups = [], {}

    def push(group, src, dst, device):
        at, slot = groups.setdefault(group, len(groups)), len(sends) % N_SEND
        if len(sends) >= N_SEND:
            sends[-N_SEND].wait_send()
        copy = pltpu.make_async_remote_copy(
            src_ref=src, dst_ref=dst, send_sem=send_sem.at[slot], recv_sem=recv_sem.at[at],
            device_id=device, device_id_type=MESH,
        )
        copy.start()
        sends.append(copy)

    def take(group, ref):
        pltpu.make_async_copy(ref, ref, recv_sem.at[groups[group]]).wait()

    own = blk(z, xl, c)
    n_loads = [0]

    def load(src, dst):
        copy = pltpu.make_async_copy(src, dst, load_sem.at[n_loads[0]])
        copy.start()
        n_loads[0] += 1
        return copy

    barrier = pltpu.get_barrier_semaphore()
    plane = [
        dev(y_=yy(i // 4), xh_=(1 - xh) if i // 2 % 2 else xh, xl_=(1 - xl) if i % 2 else xl)
        for i in range(1, 16)
    ]
    peers = [dev(z_=zz(1)), dev(z_=zz(-1)), dev(xl_=1 - xl), dev(c_=1 - c)]
    peers += [dev(y_=yy(1)), dev(y_=yy(-1)), dev(xh_=1 - xh)]
    for peer in peers:
        pl.semaphore_signal(barrier, inc=1, device_id=peer, device_id_type=MESH)

    feat_loads = [load(feat.at[:, pl.ds(h * 128, 128)], panels[h].at[own]) for h in range(2)]
    small_loads = [load(cols_in, cols), load(counts_in, counts), load(weight, w_v), load(bias_in, bias)]
    tile_loads = [load(tiles.at[b, 0], stage.at[b]) for b in range(4)]
    cot_load = load(cot, cot_v)
    for copy in feat_loads:
        copy.wait()
    pl.semaphore_wait(barrier, len(peers))

    up, down, across, twin = dev(z_=zz(1)), dev(z_=zz(-1)), dev(xl_=1 - xl), dev(c_=1 - c)
    along = {1: up, -1: down}
    both = (1, -1)
    AG_P = 128 - AG_Q
    ep_half = {1: (AG_Q, 40), -1: (AG_Q + 40, AG_P - 40)}
    eq_half = {1: (0, 32), -1: (32, AG_Q - 32)}

    def same(h, key, at, span, device):
        ref = panels[h].at[at, pl.ds(*span)]
        push((h, *key), ref, ref, device)

    def took(h, key, blocks, count):
        take((h, *key), panels[h].at[pl.ds(0, blocks), pl.ds(0, count)])

    def ag_init(h):
        same(h, ("Q", 0), own, (0, AG_Q), across)
        for d in both:
            same(h, ("EP", d, 1), own, (AG_Q, AG_P), along[d])
        for d in both:
            same(h, ("EQ", d, 1), own, (0, AG_Q), along[d])
        same(h, ("P", 0), own, (AG_Q, AG_P), across)
        same(h, ("SS",), own, (0, 128), twin)

    def ag_crossed(h, o):
        took(h, ("P", o), 1, AG_P)
        same(h, ("SS",), blk(zz(-o), 1 - xl, c), (0, 128), twin)

    def ag_e(h, k):
        for d in both:
            at = blk(zz(-d * k), xl, c)
            took(h, ("EP", d, k), 1, AG_P)
            same(h, ("EP", d, k + 1), at, (AG_Q, AG_P) if k < 3 else ep_half[d], along[d])
            same(h, ("P", d * k), at, (AG_Q, AG_P), across)
        for d in both:
            at = blk(zz(-d * k), xl, c)
            took(h, ("EQ", d, k), 1, AG_Q)
            same(h, ("EQ", d, k + 1), at, (0, AG_Q) if k < 3 else eq_half[d], along[d])
            same(h, ("SS",), at, (0, 128), twin)

    def ag_q(h, k):
        if k == 0:
            took(h, ("Q", 0), 1, AG_Q)
        for d in both:
            at = blk(zz(-d * k), 1 - xl, c)
            if k > 0:
                took(h, ("Q", d, k), 1, AG_Q)
            same(h, ("Q", d, k + 1), at, (0, AG_Q) if k < 3 else eq_half[d], along[d])

    def ag_step(h, k):
        if k < 4:
            ag_e(h, k)
        else:
            at = blk(zz(4), xl, c)
            for d in both:
                took(h, ("EP", d, 4), 1, ep_half[d][1])
            same(h, ("P", 4), at, (AG_Q, AG_P), across)
            for d in both:
                took(h, ("EQ", d, 4), 1, eq_half[d][1])
            same(h, ("SS",), at, (0, 128), twin)
        ag_q(h, k - 1)
        for o in {1: (), 2: (0,), 3: (1, -1), 4: (2, -2)}[k]:
            ag_crossed(h, o)

    def ag_end(h):
        ag_crossed(h, 3)
        ag_crossed(h, -3)
        for d in both:
            took(h, ("Q", d, 4), 1, eq_half[d][1])
        ag_crossed(h, 4)
        took(h, ("SS",), 16, 128)

    def prepare_tables():
        for copy in small_loads:
            copy.wait()
        wh, wl = split(w_v[...])
        w_hi[...] = wh
        w_lo[...] = wl

        @pl.loop(0, 64)
        def _(i):
            b, col = lax.div(i, 16), lax.rem(i, 16)
            slot, live = jnp.int32(0), jnp.float32(0)
            for t in range(6):
                hit = jnp.logical_and(cols[b, 0, t] == col, counts[0, b] > t)
                slot = jnp.where(hit, b * 6 + t, slot)
                live = jnp.where(hit, jnp.float32(1), live)
            inv[i] = slot
            msk[i] = live

    def prepare(b):
        tile_loads[b].wait()
        for t in range(6):
            hi, lo = split(stage[b, t])
            a_hi[b, :, pl.ds(t * T, T)] = hi
            a_lo[b, :, pl.ds(t * T, T)] = lo

    def forward(b):
        for t in range(6):
            at = cols[b, 0, t]
            live = jnp.where(counts[0, b] > t, jnp.float32(1), jnp.float32(0))
            for h in range(2):
                hi, lo = split(panels[h][pl.ds(2 * at, 2)].reshape(T, 128) * live)
                x_hi[pl.ds(t * T, T), pl.ds(h * 128, 128)] = hi
                x_lo[pl.ds(t * T, T), pl.ds(h * 128, 128)] = lo
        total = dot3((a_hi[b], a_lo[b]), (x_hi[...], x_lo[...]))
        for h in range(2):
            part[h, pl.ds(b * T, T), :] = total[:, h * 128 : h * 128 + 128]

    ahead, behind, opposite = dev(y_=yy(1)), dev(y_=yy(-1)), dev(xh_=1 - xh)

    def rows(b, k, first, count):
        return pl.ds(m8(b * T + yy(k) * 64 + first), count)

    def s1(h, b):
        push((h, "Y1", 1, b), part.at[h, rows(b, 2, 0, 32)], y1.at[h, b, 0], ahead)
        push((h, "Y1", -1, b), part.at[h, rows(b, 2, 32, 32)], y1.at[h, b, 1], behind)

    def s2(h, b):
        take((h, "Y1", 1, b), y1.at[h, b, 0])
        part[h, rows(b, 1, 0, 32)] += y1[h, b, 0]
        push((h, "Y2", b), part.at[h, rows(b, 1, 0, 64)], y2.at[h, b, 0], ahead)
        take((h, "Y1", -1, b), y1.at[h, b, 1])
        part[h, rows(b, -1, 32, 32)] += y1[h, b, 1]
        push((h, "Y2", b), part.at[h, rows(b, -1, 0, 64)], y2.at[h, b, 1], behind)

    def s3(h, b):
        take((h, "Y2", b), y2.at[h, b])
        ysum[h, b] = part[h, rows(b, 0, 0, 64)] + y2[h, b, 0] + y2[h, b, 1]
        push((h, "X", b), ysum.at[h, b], arx.at[h, b], opposite)

    def s4(h, b):
        take((h, "X", b), arx.at[h, b])
        agg[h, rows(b, 0, 0, 64)] = ysum[h, b] + arx[h, b]
        mine = agg.at[h, rows(b, 0, 0, 64)]
        push((h, "Y3", 1, b), mine, mine, ahead)
        push((h, "Y3", -1, b), mine, mine, behind)

    def s5(h, b):
        take((h, "Y3", 1, b), agg.at[h, pl.ds(0, 64)])
        ref = agg.at[h, rows(b, -1, 0, 32)]
        push((h, "Y4", b), ref, ref, ahead)
        take((h, "Y3", -1, b), agg.at[h, pl.ds(0, 64)])
        ref = agg.at[h, rows(b, 1, 32, 32)]
        push((h, "Y4", b), ref, ref, behind)

    def s6(h, b):
        take((h, "Y4", b), agg.at[h, pl.ds(0, 64)])

    stores = []

    def dense(b):
        span = pl.ds(b * T, T)
        summed = jnp.concatenate([agg[0, span], agg[1, span]], axis=1)
        w = (w_hi[...], w_lo[...])
        pre = dot3(split(summed), w) + bias[...]
        sigma = jax.nn.sigmoid(pre)
        hid[span, :] = pre * sigma
        stores.append(load(hid.at[span], hid_out.at[span]))
        grad = cot_v[span, :] * sigma * (1.0 + pre * (1.0 - sigma))
        gs = split(grad)
        bh, bl = split(dot3(w, gs, 1, 1))
        for t in range(6):
            tile = pl.ds(t * T, T)
            sp = dot3((bh, bl), (a_hi[b, :, tile], a_lo[b, :, tile]))
            spread[b * 6 + t, 0] = sp[:, :128]
            spread[b * 6 + t, 1] = sp[:, 128:]
        gw = dot3(split(summed.T), gs)
        gb = jnp.sum(grad, axis=0, keepdims=True)
        gw_acc[...] = gw if b == 0 else gw_acc[...] + gw
        gb_acc[...] = gb if b == 0 else gb_acc[...] + gb

    ag_init(0)
    ag_init(1)
    prepare_tables()
    for k in range(1, 5):
        for h in range(2):
            ag_step(h, k)
        prepare(k - 1)
    for h in range(2):
        ag_end(h)
    for b in range(4):
        forward(b)
        for h in range(2):
            s1(h, b)
    for stage in (s2, s3, s4, s5):
        for b in range(4):
            for h in range(2):
                stage(h, b)
    cot_load.wait()
    for b in range(4):
        for h in range(2):
            s6(h, b)
        dense(b)

    gwp[...] = jnp.zeros_like(gwp)
    for c_ in range(2):
        for xl_ in range(2):
            piece = gw_acc[pl.ds(m8(grp * 32 + (xl_ * 2 + c_) * 8), 8), :]
            gwp[c_, xl_, :, pl.ds(0, 256)] = piece * scaling
            gwp[c_, xl_, pl.ds(0, 1), pl.ds(256, 128)] = gb_acc[:, pl.ds(0, 128)] * scaling
            gwp[c_, xl_, pl.ds(1, 1), pl.ds(256, 128)] = gb_acc[:, pl.ds(128, 128)] * scaling
    push("G1", gwp.at[1 - c], g1, twin)

    chip = y * 4 + xh * 2 + xl

    def g_step(i):
        if i == 1:
            take("G1", g1)
            gwp[c] += g1[...]
            push("G2", gwp.at[c, 1 - xl], g2, across)
        elif i == 2:
            take("G2", g2)
            r3[z] = gwp[c, xl] + g2[...]
            for k in range(1, NZ):
                push("G3", r3.at[z], r3.at[z], dev(z_=zz(k)))
        elif i == 3:
            take("G3", r3.at[pl.ds(0, NZ - 1)])
            fin = r3[0]
            for k in range(1, NZ):
                fin = fin + r3[k]
            gb_out[:, pl.ds(0, 128)] = fin[0:1, 256:]
            gb_out[:, pl.ds(128, 128)] = fin[1:2, 256:]
            gwo[chip, c] = fin[:, :256]
            for peer in plane:
                push("G4", gwo.at[chip, c], gwo.at[chip, c], peer)
        elif i == 4:
            take("G4", gwo.at[pl.ds(0, 15), 0])
            push("G5", gwo.at[:, c], gwo.at[:, c], twin)

    def gather(col, half):
        total = None
        for b in range(4):
            at = b * 16 + col
            term = spread[inv[at], half] * msk[at]
            total = term if total is None else total + term
        return total

    slot_of = {o: i for i, o in enumerate((4, 3, -3, 2, -2, 1, -1, 0))}
    lane_of = {1: 0, -1: 1}
    RS_P = T - RS_Q
    p_rows, q_rows = pl.ds(RS_Q, RS_P), pl.ds(0, RS_Q)

    def col_of(o, other):
        return zz(o) * 2 + ((1 - xl) if other else xl)

    def pair_of(o):
        return pl.ds(pl.multiple_of(zz(o) * 2, 2), 2)

    def to_twin(o):
        for other in (True, False):
            col = col_of(o, other)
            g_send[col] = gather(col, 1 - c)
        push(("S", o), g_send.at[pair_of(o)], g_recv.at[pair_of(o)], twin)

    def chip_sum(o):
        take(("S", o), g_recv.at[pair_of(o)])
        for other in (True, False):
            col = col_of(o, other)
            g_own[col] = gather(col, c) + g_recv[col]
            if other:
                push(("RX", o), g_own.at[col, p_rows], rx.at[slot_of[o]], across)

    pieces = {"RQ": (True, 0, 56, lq), "REQ": (False, 0, 56, le), "REP": (False, RS_Q, 72, le)}

    def ring(name, k):
        other, first, count, land = pieces[name]
        turns = [(part, d) for part in range(2) for d in both]
        if k == 4:
            turns = [(part, d) for part, d in turns if part == lane_of[d]]
        if k == 3:
            turns.sort(key=lambda turn: turn[0] == lane_of[turn[1]])
        for part, d in turns:
            span = pl.ds(first + part * count, count)
            col = col_of(d * k, other)
            if k < 3 or (k == 3 and part == lane_of[d]):
                take((name, d, part, k + 1), land.at[lane_of[d], k, span])
                g_own[col, span] += land[lane_of[d], k, span]
            push((name, d, part, k), g_own.at[col, span], land.at[lane_of[d], k - 1, span], along[d])

    def ring_end(name, part):
        other, first, count, land = pieces[name]
        for d in both:
            take((name, d, part, 1), land.at[lane_of[d], 0, pl.ds(first + part * count, count)])

    def ring_q(k):
        ring("RQ", k)
        ring("REQ", k)

    def ring_p(k):
        for o in (4,) if k == 4 else (k, -k):
            take(("RX", o), rx.at[slot_of[o]])
            g_own[col_of(o, False), p_rows] += rx[slot_of[o]]
        ring("REP", k)

    to_twin(4)
    to_twin(3)
    to_twin(-3)
    chip_sum(4)
    ring_q(4)
    g_step(1)
    to_twin(2)
    to_twin(-2)
    chip_sum(3)
    chip_sum(-3)
    to_twin(1)
    to_twin(-1)
    to_twin(0)
    ring_p(4)
    ring_q(3)
    g_step(2)
    chip_sum(2)
    chip_sum(-2)
    ring_p(3)
    chip_sum(1)
    chip_sum(-1)
    chip_sum(0)
    ring_q(2)
    g_step(3)
    ring_p(2)
    ring_q(1)
    ring_p(1)

    far, near = col_of(0, True), col_of(0, False)
    for part in range(2):
        ring_end("RQ", part)
        span = pl.ds(part * 56, 56)
        g_own[far, span] += lq[0, 0, span] + lq[1, 0, span]
        push(("XF", part), g_own.at[far, span], xq.at[span], across)
    g_step(4)
    for part in range(2):
        ring_end("REQ", part)
    take(("RX", 0), rx.at[slot_of[0]])
    for part in range(2):
        ring_end("REP", part)
    g_own[near, p_rows] += le[0, 0, p_rows] + le[1, 0, p_rows] + rx[slot_of[0]]
    take("G5", gwo.at[:, 0])
    gw_out[...] = gwo[...].reshape(256, 256)
    for part in range(2):
        take(("XF", part), xq.at[pl.ds(part * 56, 56)])
    g_own[near, q_rows] += le[0, 0, q_rows] + le[1, 0, q_rows] + xq[...]
    gf_out[...] = g_own[near].T

    assert len(groups) == N_MSG and n_loads[0] == 15
    for store in stores:
        store.wait()
    for copy in sends[-N_SEND:]:
        copy.wait_send()


def deliver(hid, gf, gw, gb, hid_out, gf_out, gw_out, gb_out, hid_v, gf_v, gw_v, gb_v, sem_in, sem_out):
    steps = [(hid.at[pl.ds(i * T, T)], hid_v.at[pl.ds(i * T, T)], hid_out.at[pl.ds(i * T, T)]) for i in range(4)]
    steps += [(gf, gf_v, gf_out), (gw, gw_v, gw_out), (gb, gb_v, gb_out)]
    ins = [pltpu.make_async_copy(a, v, sem_in.at[i]) for i, (a, v, _) in enumerate(steps)]
    outs = [pltpu.make_async_copy(v, o, sem_out.at[i]) for i, (_, v, o) in enumerate(steps)]
    for copy in ins:
        copy.start()
    for first, then in zip(ins, outs):
        first.wait()
        then.start()
    for copy in outs:
        copy.wait()


def on_device(features, tiles, cols, counts, weight, bias, cot):
    n_rows = cot.shape[0]
    scaling = 1.0 / float(n_rows * 32) ** 0.5
    vmem = pl.BlockSpec(memory_space=pltpu.VMEM)
    hbm = pl.BlockSpec(memory_space=pl.ANY)
    shape = jax.ShapeDtypeStruct
    V = pltpu.VMEM
    scratch = [
        V((32, 128, 128), F32), V((32, 128, 128), F32),
        V((4, 6, T, T), F32),
        V((4, T, 6 * T), BF16), V((4, T, 6 * T), BF16),
        V((6 * T, T), BF16), V((6 * T, T), BF16),
        V((T, T), F32), V((T, T), BF16), V((T, T), BF16),
        V((1, T), F32),
        V((1024, T), F32),
        V((2, 1024, 128), F32),
        V((2, 4, 2, 32, 128), F32), V((2, 4, 2, 64, 128), F32),
        V((2, 4, 64, 128), F32), V((2, 4, 64, 128), F32),
        V((2, 1024, 128), F32), V((1024, T), F32),
        V((T, T), F32), V((1, T), F32),
        V((24, 2, T, 128), F32),
        V((16, T, 128), F32), V((16, T, 128), F32), V((16, T, 128), F32),
        V((8, T - RS_Q, 128), F32),
        V((2, 4, T, 128), F32), V((2, 4, RS_Q, 128), F32),
        V((RS_Q, 128), F32),
        V((2, 2, 8, 384), F32), V((2, 8, 384), F32), V((8, 384), F32),
        V((8, 8, 384), F32),
        V((16, 2, 8, T), F32),
        pltpu.SMEM((4, 1, 6), jnp.int32), pltpu.SMEM((1, 4), jnp.int32),
        pltpu.SMEM((64,), jnp.int32), pltpu.SMEM((64,), F32),
        pltpu.SemaphoreType.DMA((N_SEND,)), pltpu.SemaphoreType.DMA((N_MSG,)),
        pltpu.SemaphoreType.DMA((15,)),
    ]
    outs = (shape((1024, T), F32), shape((128, T), F32), shape((T, T), F32), shape((1, T), F32))
    results = pl.pallas_call(
        functools.partial(kernel, scaling),
        out_shape=outs,
        in_specs=[hbm] * 7,
        out_specs=(hbm, vmem, vmem, vmem),
        scratch_shapes=scratch,
        compiler_params=pltpu.CompilerParams(
            collective_id=0, has_side_effects=True, vmem_limit_bytes=60 << 20,
        ),
        name="graph_layer",
    )(features, tiles, cols, counts.T, weight, bias.reshape(1, T), cot)
    hid, gf, gw, gb = pl.pallas_call(
        deliver,
        out_shape=outs,
        in_specs=[hbm] * 4,
        out_specs=(hbm,) * 4,
        scratch_shapes=[V(o.shape, F32) for o in outs] + [pltpu.SemaphoreType.DMA((7,))] * 2,
        name="deliver",
    )(*results)
    return hid, gf, gw, gb.reshape(T)


def solution(mesh):
    return jax.shard_map(
        on_device,
        mesh=mesh,
        in_specs=(
            P(("grp", "row"), None),
            P("row", "grp", None, None, None),
            P("row", "grp", None),
            P("row", "grp"),
            P(),
            P(),
            P("row", None),
        ),
        out_specs=(P("row", None), P(("grp", "row"), None), P(), P()),
        check_vma=False,
    )
```
